32 devices in a mesh: dom: 32 (over z, y, x, core).
Axes of the slice: x: 2, y: 2, z: 4, core: 2. Of those that a mesh axis runs over, the one named last changes fastest.
Arguments:
- rest_pos: float32 [3, 131072], P(None, 'dom'), may hold values from -6 to 6
- displacement: float32 [3, 131072], P(None, 'dom'), may hold values from -3 to 3
- velocity: float32 [3, 131072], P(None, 'dom'), may hold values from -6 to 6
- ext_force: float32 [3, 131072], P(None, 'dom'), may hold values from -6 to 6
- node_mass: float32 [131072], P('dom'), may hold values from 0.5 to 2
- body_accel: float32 [3], replicated, may hold values from -2 to 2
- connectivity: int32 [8, 131072], P(None, 'dom'), may hold values from 0 to 4095
- elem_material: int32 [1024], P('dom'), may hold values from 0 to 7
- stiffness: float32 [8, 24, 24], replicated, may hold values from -1.25 to 1.25
- shared_nodes: int32 [32, 5, 128], P('dom'), may hold values from 0 to 4095, as said below
- contact_slave: int32 [65536], P('dom'), may hold values from 0 to 4095
- contact_owner: int32 [65536, 1], P('dom'), may hold values from 0 to 31; in each aligned block of 2048 rows (0 to 2047, 2048 to 4095, ...) at most 256 rows name the same one
- contact_master: int32 [65536], P('dom'), may hold values from 0 to 4095
- contact_normal: float32 [3, 65536], P(None, 'dom'), may hold values from -4 to 4
- part_of_node: int32 [131072], P('dom'), may hold values from 0 to 799
- part_mass: float32 [400], replicated, may hold values from 81 to 327
- part_center: float32 [3, 400], replicated, may hold values from -1 to 1
- part_inertia: float32 [3, 400], replicated, may hold values from 81 to 327
Outputs:
- nodal_velocity: float32 [3, 131072], P(None, 'dom')
- part_motion: float32 [6, 400], replicated
The draws below stay inside these ranges and needn't reach their ends.
Inputs may be any that keep to these rules, and one draw needn't show every extreme that they name: `connectivity`: offsets are taken modulo 4096 after adding the element's own local number. `shared_nodes`: on each partition d the 5 x 128 entries are distinct interface copies; entry k of list b on d and entry k of list b on d XOR 2**b are copies of one node. `contact_slave`: slave indices are local copies of the contact's own partition. `contact_owner`: among the 2048 contacts of one partition no owner appears more than 256 times, and some owner appears exactly 256 times. `contact_master`: master indices are local copies of the owner partition. `part_of_node`: values of 400 or more mark copies of no rigid part.
All inputs are finite; a program needn't handle non-finite values.
Results may differ from the reference program's by a relative error of at most 0.0001.
Values sent between devices are 32-bit elements; how exact they have to be, the bound alone decides.
A program may use at most 128 MiB of HBM per device.

```python
import math
import jax
import jax.numpy as jnp
import numpy as np
from jax import lax

NODE_DEV = 4096
E_DEV = 4096
SH = 128
NBR = 5
C_DEV = 2048
CAP = 256
CYCLES = 3
MATS = 8
PARTS_SIZE = 400
DOMS = 32
NODES = 131072
ELEMS = 131072
BLOCKS = 1024
CONTACTS = 65536


def draw_shared_nodes(key, part):
    domain_keys = jax.random.split(key, DOMS)
    orders = jax.vmap(lambda one_key: jax.random.permutation(one_key, NODE_DEV))(domain_keys)
    return orders[:, :NBR * SH].reshape(DOMS, NBR, SH).astype(jnp.int32)


def with_ends(drawn, stream_key, low, largest):
    longest = drawn.shape.index(max(drawn.shape))
    spots = []
    for shift in (0, 1):
        where = [jax.random.randint(jax.random.fold_in(stream_key, axis), (), 0, length) for axis, length in enumerate(drawn.shape)]
        where[longest] = (where[longest] + shift) % drawn.shape[longest]
        spots.append(tuple(where))
    return drawn.at[spots[0]].set(low).at[spots[1]].set(largest)


def levels(key, shape, cuts, smallest, largest):
    level = 1.0
    for dim, shards_of in cuts:
        steps = jax.random.uniform(jax.random.fold_in(jax.random.fold_in(key, 6), dim), (shards_of,), jnp.float32, smallest / len(cuts), largest / len(cuts))
        level = level * jnp.repeat(jnp.exp(steps), shape[dim] // shards_of).reshape((-1,) + (1,) * (len(shape) - 1 - dim))
    return level


def assign_block(key, own, number, rows, count, top, bound, lean):
    ranking = jax.random.permutation(key, count)
    heavy_load, common = load_shares(count, rows * top, bound, lean, True), load_shares(count, rows * top, bound, lean, False)
    places = jnp.arange(count)

    def named(tallies, rotation):
        used = int((tallies > 0).sum())
        fixed = max(1, used // 4)
        shifted = fixed + (places - fixed + rotation * (used - fixed)) % max(1, count - fixed)
        return jnp.zeros((count,), jnp.int32).at[ranking[jnp.where(places < fixed, places, shifted)]].set(jnp.asarray(tallies, jnp.int32))

    tallies = jnp.where(number % 4 == 0, named(heavy_load, number // 4), named(common, number - number // 4 - 1))
    mixed = jax.random.permutation(jax.random.fold_in(own, 3), count)
    donor, receiver = mixed[0:count // 2 * 2:2], mixed[1:count // 2 * 2:2]
    slack = jnp.minimum(tallies[donor] - 1, bound - tallies[receiver]) // 2
    slack = jnp.where((donor == ranking[0]) | (receiver == ranking[0]) | (tallies[receiver] == 0), 0, jnp.maximum(slack, 0))
    shifted = jax.random.randint(jax.random.fold_in(own, 4), (count // 2,), 0, 1 << 20) % (slack + 1)
    tallies = tallies.at[donor].add(-shifted).at[receiver].add(shifted)
    labels = jnp.searchsorted(jnp.cumsum(tallies), jnp.arange(rows * top), side="right").astype(jnp.int32)
    listing = labels.reshape(top, rows).T
    listing = listing[jax.random.permutation(jax.random.fold_in(own, 1), rows)]
    rotation = jax.random.randint(jax.random.fold_in(own, 2), (rows, 1), 0, top)
    return jnp.take_along_axis(listing, (jnp.arange(top)[None, :] + rotation) % top, axis=1)


def load_shares(amount, total, most, lean, full):
    loads = [(1 << 20) // math.isqrt(standing ** lean) + 1 for standing in range(1, amount + 1)]
    largest = most if full else min(most, max(-(-total // amount), total * loads[0] // sum(loads)))
    least = 1 if total - largest >= amount - 1 else 0
    given, surplus = [largest] + [least] * (amount - 1), total - largest - least * (amount - 1)
    while surplus > 0:
        movable = [i for i in range(1, amount) if given[i] < largest] or [i for i in range(1, amount) if given[i] < most]
        pool, budget = sum([loads[i] for i in movable]), surplus
        for i in movable:
            more = min(most - given[i], max(1, budget * loads[i] // pool), surplus)
            given[i] = given[i] + more
            surplus = surplus - more
    return np.array(given)


def centred(rng, shape, spread, bound, cuts=(), kind=jnp.bfloat16):
    result = spread * jax.random.normal(rng, shape, jnp.float32)
    if cuts:
        result = result * levels(rng, shape, cuts, -0.22, 0.18)
    return jnp.clip(result, -bound, bound).astype(kind)


def setup_inputs(seed: int = 0) -> dict:
    keys = jax.random.split(jax.random.key(seed), 19)
    rest_pos = centred(keys[0], (3, NODES), 1.0, 6.0, ((1, 32),), jnp.float32)
    displacement = centred(keys[1], (3, NODES), 0.2, 3.0, ((1, 32),), jnp.float32)
    velocity = centred(keys[2], (3, NODES), 1.0, 6.0, ((1, 32),), jnp.float32)
    ext_force = centred(keys[3], (3, NODES), 1.0, 6.0, ((1, 32),), jnp.float32)
    node_mass = jnp.clip(jnp.exp(math.log(2.0) - 1.3862944 * jax.random.uniform(keys[4], (NODES,), jnp.float32) ** levels(keys[4], (NODES,), ((0, 32),), -0.2, 0.2)), 0.5, 2.0)
    body_accel = jnp.clip(jax.random.uniform(keys[5], (3,), jnp.float32, -2.0, 2.0), -2.0, 2.0)
    connectivity = with_ends(jax.random.randint(keys[6], (8, ELEMS), 0, min(NODE_DEV, 16368)), jax.random.fold_in(keys[6], 1), 0, (min(NODE_DEV, 16368)) - 1).astype(jnp.int32)
    elem_material = with_ends(jax.random.randint(keys[7], (BLOCKS,), 0, MATS), jax.random.fold_in(keys[7], 1), 0, MATS - 1).astype(jnp.int32)
    stiffness = centred(keys[8], (MATS, 24, 24), 24 ** -0.5, 1.25, (), jnp.float32)
    shared_nodes = draw_shared_nodes(jax.random.fold_in(keys[18], 71), 0)
    contact_slave = with_ends(jax.random.randint(keys[10], (CONTACTS,), 0, NODE_DEV), jax.random.fold_in(keys[10], 1), 0, NODE_DEV - 1).astype(jnp.int32)
    contact_owner_keys = jax.random.split(jax.random.fold_in(keys[11], 1), CONTACTS // C_DEV)
    contact_owner_turns = jax.random.permutation(jax.random.fold_in(keys[11], 3), CONTACTS // C_DEV)
    contact_owner = jax.vmap(lambda own, number: assign_block(jax.random.fold_in(keys[11], 2), own, number, C_DEV, DOMS, 1, CAP, 2))(contact_owner_keys, contact_owner_turns).reshape((CONTACTS, 1))
    contact_master = with_ends(jax.random.randint(keys[12], (CONTACTS,), 0, NODE_DEV), jax.random.fold_in(keys[12], 1), 0, NODE_DEV - 1).astype(jnp.int32)
    contact_normal = centred(keys[13], (3, CONTACTS), 0.6, 4.0, ((1, 32),), jnp.float32)
    part_of_node = with_ends(jax.random.randint(keys[14], (NODES,), 0, 2 * PARTS_SIZE), jax.random.fold_in(keys[14], 1), 0, (2 * PARTS_SIZE) - 1).astype(jnp.int32)
    part_mass = jnp.clip(jnp.exp(jax.random.uniform(keys[15], (PARTS_SIZE,), jnp.float32, math.log(81.0), math.log(327.0))), 81.0, 327.0)
    part_center = jnp.clip(jax.random.uniform(keys[16], (3, PARTS_SIZE), jnp.float32, -1.0, 1.0), -1.0, 1.0)
    part_inertia = jnp.clip(jnp.exp(jax.random.uniform(keys[17], (3, PARTS_SIZE), jnp.float32, math.log(81.0), math.log(327.0))), 81.0, 327.0)
    return dict(rest_pos=rest_pos, displacement=displacement, velocity=velocity, ext_force=ext_force, node_mass=node_mass, body_accel=body_accel, connectivity=connectivity, elem_material=elem_material, stiffness=stiffness, shared_nodes=shared_nodes, contact_slave=contact_slave, contact_owner=contact_owner, contact_master=contact_master, contact_normal=contact_normal, part_of_node=part_of_node, part_mass=part_mass, part_center=part_center, part_inertia=part_inertia)


TIME_STEP = 0.1
DAMP_RATIO = 0.05
PENALTY = 2.0
GAP_WIDTH = 0.5
CONTACT_DAMP = 0.2


def element_forces(corners, material, stiffness, nodal_field):
    blocks = corners.shape[1] // 128
    gathered = nodal_field[:, corners].reshape(24, blocks, 128)
    block_matrix = stiffness[material]
    forces = jnp.einsum("bij,jbk->ibk", block_matrix, gathered, precision=lax.Precision.HIGHEST)
    return jnp.zeros_like(nodal_field).at[:, corners.reshape(-1)].add(forces.reshape(3, 8 * corners.shape[1]))


def contact_push(slave_pos, slave_vel, master_pos, master_vel, normal):
    gap_size = jnp.sum((slave_pos - master_pos) * normal, axis=0)
    closing = jnp.sum((slave_vel - master_vel) * normal, axis=0)
    push_size = PENALTY * GAP_WIDTH * jax.nn.softplus(-gap_size / GAP_WIDTH) - CONTACT_DAMP * closing
    return push_size[None] * normal


def cross_product(left, right):
    return jnp.stack([left[1] * right[2] - left[2] * right[1], left[2] * right[0] - left[0] * right[2], left[0] * right[1] - left[1] * right[0]])


def by_domain(array_in):
    return array_in.reshape(array_in.shape[0], DOMS, NODE_DEV).transpose(1, 0, 2)


def to_global(array_in):
    return array_in.transpose(1, 0, 2).reshape(array_in.shape[1], NODES)


def take_columns(values_one, index_one):
    return values_one[:, index_one]


def add_columns(values_one, index_one, added_one):
    return values_one.at[:, index_one].add(added_one)


def reference(rest_pos, displacement, velocity, ext_force, node_mass, body_accel, connectivity, elem_material, stiffness, shared_nodes, contact_slave, contact_owner, contact_master, contact_normal, part_of_node, part_mass, part_center, part_inertia):
    displaced = by_domain(displacement)
    speeds = by_domain(velocity)
    applied = by_domain(ext_force)
    masses = node_mass.reshape(DOMS, 1, NODE_DEV)
    local_elem = jnp.arange(E_DEV, dtype=jnp.int32)
    corners = (connectivity.reshape(8, DOMS, E_DEV).transpose(1, 0, 2) + local_elem[None, None, :]) % NODE_DEV
    material = elem_material.reshape(DOMS, E_DEV // 128)
    shared_flat = shared_nodes.reshape(DOMS, NBR * SH)
    domain_ids = jnp.arange(DOMS, dtype=jnp.int32)
    accel_column = body_accel[None, :, None]

    def one_domain(inputs):
        return element_forces(inputs[0], inputs[1], stiffness, inputs[2])

    assembled = jnp.zeros_like(displaced)
    for cycle_index in range(CYCLES):
        internal = lax.map(one_domain, (corners, material, displaced + DAMP_RATIO * speeds))
        own_values = jax.vmap(take_columns)(internal, shared_flat).reshape(DOMS, 3, NBR, SH)
        pieces = [own_values[domain_ids ^ (1 << bit_number), :, bit_number] for bit_number in range(NBR)]
        received = jnp.stack(pieces, axis=2).reshape(DOMS, 3, NBR * SH)
        assembled = jax.vmap(add_columns)(internal, shared_flat, received)
        speeds = speeds + TIME_STEP * ((applied - assembled) / masses - accel_column)
        displaced = displaced + TIME_STEP * speeds

    positions = to_global(by_domain(rest_pos) + displaced)
    speeds_all = to_global(speeds)
    last_internal = to_global(assembled)
    contact_domain = jnp.arange(CONTACTS, dtype=jnp.int32) // C_DEV
    slave_node = contact_domain * NODE_DEV + contact_slave
    master_node = contact_owner[:, 0] * NODE_DEV + contact_master
    pushed = contact_push(positions[:, slave_node], speeds_all[:, slave_node], positions[:, master_node], speeds_all[:, master_node], contact_normal)
    contact = jnp.zeros_like(positions).at[:, slave_node].add(pushed).at[:, master_node].add(-pushed)
    nodal_velocity = speeds_all + TIME_STEP * contact / node_mass[None]
    net_force = ext_force - last_internal + contact - node_mass[None] * body_accel[:, None]

    part_index = jnp.minimum(part_of_node, PARTS_SIZE)

    def segment_rows(columns_in):
        return jax.ops.segment_sum(columns_in.T, part_index, PARTS_SIZE + 1)[:PARTS_SIZE].T

    mass_moments = segment_rows(jnp.concatenate([node_mass[None], node_mass[None] * positions], 0))
    mass_total = part_mass + mass_moments[0]
    centre = (part_mass[None] * part_center + mass_moments[1:4]) / mass_total[None]
    centre_ext = jnp.concatenate([centre, jnp.zeros((3, 1), centre.dtype)], 1)
    lever_arm = positions - centre_ext[:, part_index]
    load_sums = segment_rows(jnp.concatenate([net_force, cross_product(lever_arm, net_force)], 0))
    part_motion = jnp.concatenate([load_sums[0:3] / mass_total[None], load_sums[3:6] / part_inertia], 0)
    return nodal_velocity, part_motion
```

```python
import functools

import jax
import jax.numpy as jnp
from jax import lax
from jax.experimental import pallas as pl
from jax.experimental.pallas import tpu as pltpu
from jax.sharding import PartitionSpec as P

CYCLES = 3
PARTS_SIZE = 400
TIME_STEP = 0.1
DAMP_RATIO = 0.05
PENALTY = 2.0
GAP_WIDTH = 0.5
CONTACT_DAMP = 0.2
L = 128
F32 = jnp.float32
BF16 = jnp.bfloat16
NT = (((1,), (1,)), ((), ()))


def split_pieces(value, pieces):
    out = []
    for _ in range(pieces):
        piece = value.astype(BF16)
        out.append(piece)
        value = value - piece.astype(F32)
    return out


def row_of(value, row, count):
    return jnp.broadcast_to(value[row : row + 1, :], (count, L))


def lookup(tables, index):
    high = index >> 7
    low = index & 127
    found = [None] * len(tables[0])
    for r, rows in enumerate(tables):
        hit = high == r
        for c, row in enumerate(rows):
            got = jnp.take_along_axis(
                jnp.broadcast_to(row, index.shape), low, axis=1, mode="promise_in_bounds"
            )
            found[c] = got if found[c] is None else jnp.where(hit, got, found[c])
    return found


def table_rows(refs, rows):
    return [[ref(r) for ref in refs] for r in range(rows)]


def scatter_tile(index, values, rows, pieces, live=None):
    high = index >> 7
    low = index & 127
    sublane = lax.broadcasted_iota(jnp.int32, (rows, L), 0)
    place = lax.broadcasted_iota(jnp.int32, (L, L), 0)
    left, right = [], []
    for s in range(live or index.shape[0]):
        mine = sublane == row_of(high, s, rows)
        stack = []
        for value in values:
            spread = jnp.where(mine, row_of(value, s, rows), 0.0)
            stack += split_pieces(spread, pieces)
        left.append(jnp.concatenate(stack, 0))
        right.append(jnp.where(place == row_of(low, s, L), 1.0, 0.0).astype(BF16))
    return lax.dot_general(
        jnp.concatenate(left, 1), jnp.concatenate(right, 1), NT, preferred_element_type=F32
    )


def unstack(total, count, rows, pieces):
    out = []
    for c in range(count):
        base = c * pieces * rows
        value = total[base : base + rows]
        for p in range(1, pieces):
            value = value + total[base + p * rows : base + (p + 1) * rows]
        out.append(value)
    return out


def advance(u, v, internal, received, shared, ext, mass, accel, rows, neighbours):
    added = unstack(scatter_tile(shared, received, rows, 3, neighbours), 3, rows, 3)
    assembled = [internal[c] + added[c] for c in range(3)]
    v = [v[c] + TIME_STEP * ((ext[c] - assembled[c]) / mass - accel[c]) for c in range(3)]
    u = [u[c] + TIME_STEP * v[c] for c in range(3)]
    return u, v, assembled


def elem_body(first, neighbours, *refs):
    if first:
        u_ref, v_ref, corner_ref, shared_ref, matrix_ref, out_ref, own_ref, field, total = refs
        u = [u_ref[c] for c in range(3)]
        v = [v_ref[c] for c in range(3)]
    else:
        (u_ref, v_ref, corner_ref, shared_ref, matrix_ref, int_ref, rec_ref, ext_ref, mass_ref,
         accel_ref, out_ref, own_ref, un_ref, vn_ref, field, total) = refs
        rows = u_ref.shape[1]
        u, v, _ = advance(
            [u_ref[c] for c in range(3)], [v_ref[c] for c in range(3)],
            [int_ref[c] for c in range(3)], [rec_ref[c] for c in range(3)], shared_ref[...],
            [ext_ref[c] for c in range(3)], mass_ref[...], [accel_ref[c] for c in range(3)],
            rows, neighbours)
        for c in range(3):
            un_ref[c] = u[c]
            vn_ref[c] = v[c]
    rows = u_ref.shape[1]
    for c in range(3):
        field[c] = u[c] + DAMP_RATIO * v[c]
    total[...] = jnp.zeros_like(total)
    blocks = corner_ref.shape[1] // L

    def step(b, carry):
        index = corner_ref[:, pl.ds(pl.multiple_of(b * L, L), L)]
        found = lookup(
            table_rows([lambda r, c=c: field[c, r : r + 1, :] for c in range(3)], rows), index)
        g = jnp.concatenate(found, 0)
        g_hi = g.astype(BF16).astype(F32)
        rhs = jnp.concatenate([g_hi, g - g_hi, g_hi, jnp.zeros((8, L), F32)], 0).astype(BF16)
        h = jnp.dot(matrix_ref[b], rhs, preferred_element_type=F32)
        total[...] += scatter_tile(index, [h[0:8], h[8:16], h[16:24]], rows, 2)
        return carry

    lax.fori_loop(0, blocks, step, 0, unroll=2)
    internal = unstack(total[...], 3, rows, 2)
    for c in range(3):
        out_ref[c] = internal[c]
        field[c] = internal[c]
    own = lookup(
        table_rows([lambda r, c=c: field[c, r : r + 1, :] for c in range(3)], rows),
        shared_ref[...])
    for c in range(3):
        own_ref[c] = own[c]


def slots_body(owner_ref, master_ref, normal_ref, slot_ref, pay_ref, *, domains, cap):
    tiles = owner_ref.shape[0]
    slot_rows = pay_ref.shape[1]
    domain = lax.broadcasted_iota(jnp.int32, (domains, L), 0)
    tri = (lax.broadcasted_iota(jnp.int32, (L, L), 0) <= lax.broadcasted_iota(
        jnp.int32, (L, L), 1)).astype(F32).astype(BF16)
    seen = jnp.zeros((domains, 1), F32)
    for t in range(tiles):
        owner = owner_ref[t : t + 1, :]
        hit = domain == jnp.broadcast_to(owner, (domains, L))
        hits = jnp.where(hit, 1.0, 0.0)
        upto = jnp.dot(hits.astype(BF16), tri, preferred_element_type=F32) + seen
        rank = jnp.sum(jnp.where(hit, upto, 0.0), axis=0, keepdims=True) - 1.0
        slot_ref[t : t + 1, :] = owner * cap + rank.astype(jnp.int32)
        seen = seen + jnp.sum(hits, axis=1, keepdims=True)
    acc = None
    for t in range(0, tiles, 8):
        sl = slice(t, t + 8)
        values = [normal_ref[c, sl, :] for c in range(3)] + [master_ref[sl, :].astype(F32) + 1.0]
        got = scatter_tile(slot_ref[sl, :], values, slot_rows, 3)
        acc = got if acc is None else acc + got
    for c, value in enumerate(unstack(acc, 4, slot_rows, 3)):
        pay_ref[c] = value


def project_body(neighbours, u_ref, v_ref, shared_ref, int_ref, rec_ref, ext_ref, mass_ref,
                 accel_ref, rest_ref, slave_ref, slot_ref, normal_ref, x_ref, vn_ref, as_ref,
                 pay_ref):
    rows = u_ref.shape[1]
    slot_rows = pay_ref.shape[1]
    u, v, assembled = advance(
        [u_ref[c] for c in range(3)], [v_ref[c] for c in range(3)],
        [int_ref[c] for c in range(3)], [rec_ref[c] for c in range(3)], shared_ref[...],
        [ext_ref[c] for c in range(3)], mass_ref[...], [accel_ref[c] for c in range(3)],
        rows, neighbours)
    for c in range(3):
        x_ref[c] = rest_ref[c] + u[c]
        vn_ref[c] = v[c]
        as_ref[c] = assembled[c]
    acc = None
    for t in range(0, slave_ref.shape[0], 8):
        sl = slice(t, t + 8)
        found = lookup(state_rows(x_ref, vn_ref, rows), slave_ref[sl, :])
        normal = [normal_ref[c, sl, :] for c in range(3)]
        along = sum(found[c] * normal[c] for c in range(3))
        speed = sum(found[3 + c] * normal[c] for c in range(3))
        got = scatter_tile(slot_ref[sl, :], [along, speed], slot_rows, 3)
        acc = got if acc is None else acc + got
    for c, value in enumerate(unstack(acc, 2, slot_rows, 3)):
        pay_ref[c] = value


def state_rows(x_ref, v_ref, rows):
    return table_rows(
        [lambda r, c=c: x_ref[c, r : r + 1, :] for c in range(3)]
        + [lambda r, c=c: v_ref[c, r : r + 1, :] for c in range(3)], rows)


def push_body(x_ref, v_ref, early_ref, late_ref, push_ref, force_ref, total):
    rows = x_ref.shape[1]
    total[...] = jnp.zeros_like(total)

    def step(i, carry):
        sl = pl.ds(pl.multiple_of(i * 8, 8), 8)
        coded = early_ref[3, sl, :]
        master = jnp.maximum(coded - 0.5, 0.0).astype(jnp.int32)
        normal = [early_ref[c, sl, :] for c in range(3)]
        found = lookup(state_rows(x_ref, v_ref, rows), master)
        gap = late_ref[0, sl, :] - sum(found[c] * normal[c] for c in range(3))
        closing = late_ref[1, sl, :] - sum(found[3 + c] * normal[c] for c in range(3))
        z = -gap / GAP_WIDTH
        soft = jnp.maximum(z, 0.0) + jnp.log1p(jnp.exp(-jnp.abs(z)))
        push = PENALTY * GAP_WIDTH * soft - CONTACT_DAMP * closing
        push = jnp.where(coded > 0.5, push, 0.0)
        push_ref[sl, :] = push
        total[...] += scatter_tile(master, [-push * normal[c] for c in range(3)], rows, 2)
        return carry

    lax.fori_loop(0, push_ref.shape[0] // 8, step, 0)
    for c, value in enumerate(unstack(total[...], 3, rows, 2)):
        force_ref[c] = value


def finish_body(x_ref, v_ref, as_ref, ext_ref, mass_ref, accel_ref, force_ref, push_ref, slot_ref,
                slave_ref, normal_ref, part_ref, nv_ref, sums_ref, vals, total):
    rows = x_ref.shape[1]
    push_rows = [[push_ref[r : r + 1, :]] for r in range(push_ref.shape[0])]
    acc = None
    for t in range(0, slave_ref.shape[0], 8):
        sl = slice(t, t + 8)
        push = lookup(push_rows, slot_ref[sl, :])[0]
        got = scatter_tile(slave_ref[sl, :], [push * normal_ref[c, sl, :] for c in range(3)],
                           rows, 2)
        acc = got if acc is None else acc + got
    slave_force = unstack(acc, 3, rows, 2)
    mass = mass_ref[...]
    x = [x_ref[c] for c in range(3)]
    net = []
    for c in range(3):
        force = force_ref[c] + slave_force[c]
        nv_ref[c] = v_ref[c] + TIME_STEP * force / mass
        net.append(ext_ref[c] - as_ref[c] + force - mass * accel_ref[c])
    turned = [x[1] * net[2] - x[2] * net[1], x[2] * net[0] - x[0] * net[2],
              x[0] * net[1] - x[1] * net[0]]
    for i, value in enumerate([mass] + [mass * x[c] for c in range(3)] + net + turned):
        vals[i] = value
    part_rows = sums_ref.shape[1]
    total[...] = jnp.zeros_like(total)

    def step(i, carry):
        sl = pl.ds(pl.multiple_of(i * 8, 8), 8)
        part = part_ref[sl, :]
        total[...] += scatter_tile(part, [vals[k, sl, :] for k in range(10)], part_rows, 3)
        return carry

    lax.fori_loop(0, rows // 8, step, 0)
    for k, value in enumerate(unstack(total[...], 10, part_rows, 3)):
        sums_ref[k] = value


VMEM = pl.BlockSpec(memory_space=pltpu.VMEM)
SMEM = pl.BlockSpec(memory_space=pltpu.SMEM)


def call(body, outs, scratch, specs, name):
    return pl.pallas_call(
        body,
        out_shape=outs,
        in_specs=specs,
        out_specs=[VMEM] * len(outs),
        scratch_shapes=scratch,
        name=name,
        compiler_params=pltpu.CompilerParams(vmem_limit_bytes=48 * 2**20),
    )


def cross_product(left, right):
    return jnp.stack([
        left[1] * right[2] - left[2] * right[1],
        left[2] * right[0] - left[0] * right[2],
        left[0] * right[1] - left[1] * right[0],
    ])


def partner(block, axis, apart):
    count = lax.axis_size(axis)
    route = []
    for low in range(count):
        high = low | 1 << apart
        if high != low and high < count:
            route += [(low, high), (high, low)]
    return lax.ppermute(block, axis, route)


def f32(*shape):
    return jax.ShapeDtypeStruct(shape, F32)


def swap(payload, domains, cap):
    count = payload.shape[0]
    return lax.all_to_all(
        payload.reshape(count, domains, cap), "dom", split_axis=1, concat_axis=1, tiled=True
    ).reshape(payload.shape)


def per_device(rest_pos, displacement, velocity, ext_force, node_mass, body_accel, connectivity,
               elem_material, stiffness, shared_nodes, contact_slave, contact_owner,
               contact_master, contact_normal, part_of_node, part_mass, part_center,
               part_inertia):
    domains = lax.axis_size("dom")
    neighbours, shared_count = shared_nodes.shape[1:]
    nodes = displacement.shape[1]
    rows = nodes // L
    elems = connectivity.shape[1]
    blocks = elems // L
    contacts = contact_slave.shape[0]
    tiles = contacts // L
    cap = -(-(4 * contacts // domains) // L) * L
    slot_rows = domains * cap // L
    part_rows = -(-PARTS_SIZE // L)

    corners = (connectivity + jnp.arange(elems, dtype=jnp.int32)[None, :]) % nodes
    u = displacement.reshape(3, rows, L)
    v = velocity.reshape(3, rows, L)
    ext = ext_force.reshape(3, rows, L)
    rest = rest_pos.reshape(3, rows, L)
    mass = node_mass.reshape(rows, L)
    shared = jnp.concatenate(
        [shared_nodes[0], jnp.zeros((8 - neighbours, shared_count), jnp.int32)], 0)
    k_hi = lax.reduce_precision(stiffness, 8, 7)
    k_lo = stiffness - k_hi
    matrix = jnp.concatenate(
        [k_hi, k_hi, k_lo, jnp.zeros(stiffness.shape[:2] + (8,), F32)], 2).astype(BF16)
    materials = stiffness.shape[0]
    pick = (elem_material[:, None] == jnp.arange(materials, dtype=jnp.int32)[None]).astype(BF16)
    matrix = jnp.dot(pick, matrix.reshape(materials, -1), preferred_element_type=F32)
    matrix = matrix.astype(BF16).reshape(blocks, 24, 80)

    owner = contact_owner.reshape(tiles, L)
    master = contact_master.reshape(tiles, L)
    slave = contact_slave.reshape(tiles, L)
    normal = contact_normal.reshape(3, tiles, L)
    slot, early = call(
        functools.partial(slots_body, domains=domains, cap=cap),
        [jax.ShapeDtypeStruct((tiles, L), jnp.int32), f32(4, slot_rows, L)], [],
        [VMEM] * 3, "slots")(owner, master, normal)
    early = swap(early, domains, cap)

    node_shape = f32(3, rows, L)
    own_shape = f32(3, 8, L)
    scratch = [pltpu.VMEM((3, rows, L), F32), pltpu.VMEM((6 * rows, L), F32)]
    received = internal = None
    for cycle in range(CYCLES):
        if cycle == 0:
            internal, own = call(
                functools.partial(elem_body, True, neighbours), [node_shape, own_shape], scratch,
                [VMEM] * 5, "elements")(u, v, corners, shared, matrix)
        else:
            internal, own, u, v = call(
                functools.partial(elem_body, False, neighbours),
                [node_shape, own_shape, node_shape, node_shape], scratch,
                [VMEM] * 9 + [SMEM], "elements")(
                    u, v, corners, shared, matrix, internal, received, ext, mass, body_accel)
        pieces = [partner(own[:, b], "dom", b) for b in range(neighbours)]
        received = jnp.stack(pieces + [jnp.zeros_like(pieces[0])] * (8 - neighbours), axis=1)

    x, v, assembled, late = call(
        functools.partial(project_body, neighbours),
        [node_shape, node_shape, node_shape, f32(2, slot_rows, L)], [],
        [VMEM] * 7 + [SMEM] + [VMEM] * 4, "project")(
            u, v, shared, internal, received, ext, mass, body_accel, rest, slave, slot, normal)
    late = swap(late, domains, cap)
    push, force = call(
        push_body, [f32(slot_rows, L), node_shape], [pltpu.VMEM((6 * rows, L), F32)],
        [VMEM] * 4, "push")(x, v, early, late)
    push = swap(push[None], domains, cap)[0]
    nodal_velocity, sums = call(
        finish_body, [node_shape, f32(10, part_rows, L)],
        [pltpu.VMEM((10, rows, L), F32), pltpu.VMEM((30 * part_rows, L), F32)],
        [VMEM] * 5 + [SMEM] + [VMEM] * 6, "finish")(
            x, v, assembled, ext, mass, body_accel, force, push, slot, slave, normal,
            part_of_node.reshape(rows, L))
    totals = lax.psum(sums, "dom").reshape(10, part_rows * L)[:, :PARTS_SIZE]
    mass_total = part_mass + totals[0]
    centre = (part_mass[None] * part_center + totals[1:4]) / mass_total[None]
    force_sum = totals[4:7]
    torque = totals[7:10] - cross_product(centre, force_sum)
    part_motion = jnp.concatenate([force_sum / mass_total[None], torque / part_inertia], 0)
    return nodal_velocity.reshape(3, nodes), part_motion


def solution(mesh):
    placed = (
        P(None, "dom"), P(None, "dom"), P(None, "dom"), P(None, "dom"), P("dom"), P(),
        P(None, "dom"), P("dom"), P(), P("dom", None, None), P("dom"), P("dom", None), P("dom"),
        P(None, "dom"), P("dom"), P(), P(), P(),
    )
    return jax.shard_map(
        per_device, mesh=mesh, in_specs=placed, out_specs=(P(None, "dom"), P()), check_vma=False
    )
```

```python
import functools

import jax
import jax.numpy as jnp
from jax import lax
from jax.experimental import pallas as pl
from jax.experimental.pallas import tpu as pltpu
from jax.sharding import PartitionSpec as P

CYCLES = 3
PARTS_SIZE = 400
TIME_STEP = 0.1
DAMP_RATIO = 0.05
PENALTY = 2.0
GAP_WIDTH = 0.5
CONTACT_DAMP = 0.2
L = 128
F32 = jnp.float32
BF16 = jnp.bfloat16
NT = (((1,), (1,)), ((), ()))


def split_pieces(value, pieces):
    out = []
    for _ in range(pieces):
        piece = value.astype(BF16)
        out.append(piece)
        value = value - piece.astype(F32)
    return out


def row_of(value, row, count):
    return jnp.broadcast_to(value[row : row + 1, :], (count, L))


def lookup(tables, index):
    high = index >> 7
    low = index & 127
    found = [None] * len(tables[0])
    for r, rows in enumerate(tables):
        hit = high == r
        for c, row in enumerate(rows):
            got = jnp.take_along_axis(
                jnp.broadcast_to(row, index.shape), low, axis=1, mode="promise_in_bounds"
            )
            found[c] = got if found[c] is None else jnp.where(hit, got, found[c])
    return found


def table_rows(refs, rows):
    return [[ref(r) for ref in refs] for r in range(rows)]


def scatter_tile(index, values, rows, pieces, live=None):
    high = index >> 7
    low = index & 127
    sublane = lax.broadcasted_iota(jnp.int32, (rows, L), 0)
    place = lax.broadcasted_iota(jnp.int32, (L, L), 0)
    left, right = [], []
    for s in range(live or index.shape[0]):
        mine = sublane == row_of(high, s, rows)
        stack = []
        for value in values:
            row = value[s] if isinstance(value, list) else value[s : s + 1, :]
            spread = jnp.where(mine, jnp.broadcast_to(row, (rows, L)), 0.0)
            stack += split_pieces(spread, pieces)
        left.append(jnp.concatenate(stack, 0))
        right.append(jnp.where(place == row_of(low, s, L), 1.0, 0.0).astype(BF16))
    return lax.dot_general(
        jnp.concatenate(left, 1), jnp.concatenate(right, 1), NT, preferred_element_type=F32
    )


def unstack(total, count, rows, pieces):
    out = []
    for c in range(count):
        base = c * pieces * rows
        value = total[base : base + rows]
        for p in range(1, pieces):
            value = value + total[base + p * rows : base + (p + 1) * rows]
        out.append(value)
    return out


def advance(u, v, internal, received, shared, ext, mass, accel, rows, neighbours):
    added = unstack(scatter_tile(shared, received, rows, 3, neighbours), 3, rows, 3)
    assembled = [internal[c] + added[c] for c in range(3)]
    v = [v[c] + TIME_STEP * ((ext[c] - assembled[c]) / mass - accel[c]) for c in range(3)]
    u = [u[c] + TIME_STEP * v[c] for c in range(3)]
    return u, v, assembled


def by_part(rec_ref):
    return [[rec_ref[b, c : c + 1, :] for b in range(rec_ref.shape[0])] for c in range(3)]


def elem_body(first, neighbours, *refs):
    if first:
        u_ref, v_ref, corner_ref, shared_ref, matrix_ref, out_ref, own_ref, field, total = refs
        u = [u_ref[c] for c in range(3)]
        v = [v_ref[c] for c in range(3)]
    else:
        (u_ref, v_ref, corner_ref, shared_ref, matrix_ref, int_ref, rec_ref, ext_ref, mass_ref,
         accel_ref, out_ref, own_ref, un_ref, vn_ref, field, total) = refs
        rows = u_ref.shape[1]
        u, v, _ = advance(
            [u_ref[c] for c in range(3)], [v_ref[c] for c in range(3)],
            [int_ref[c] for c in range(3)], by_part(rec_ref), shared_ref[...],
            [ext_ref[c] for c in range(3)], mass_ref[...], [accel_ref[c] for c in range(3)],
            rows, neighbours)
        for c in range(3):
            un_ref[c] = u[c]
            vn_ref[c] = v[c]
    rows = u_ref.shape[1]
    for c in range(3):
        field[c] = u[c] + DAMP_RATIO * v[c]
    total[...] = jnp.zeros_like(total)
    blocks = corner_ref.shape[1] // L

    def step(b, carry):
        index = corner_ref[:, pl.ds(pl.multiple_of(b * L, L), L)]
        found = lookup(
            table_rows([lambda r, c=c: field[c, r : r + 1, :] for c in range(3)], rows), index)
        g = jnp.concatenate(found, 0)
        g_hi = g.astype(BF16).astype(F32)
        rhs = jnp.concatenate([g_hi, g - g_hi, g_hi, jnp.zeros((8, L), F32)], 0).astype(BF16)
        h = jnp.dot(matrix_ref[b], rhs, preferred_element_type=F32)
        total[...] += scatter_tile(index, [h[0:8], h[8:16], h[16:24]], rows, 2)
        return carry

    lax.fori_loop(0, blocks, step, 0, unroll=2)
    internal = unstack(total[...], 3, rows, 2)
    for c in range(3):
        out_ref[c] = internal[c]
        field[c] = internal[c]
    own = lookup(
        table_rows([lambda r, c=c: field[c, r : r + 1, :] for c in range(3)], rows),
        shared_ref[...])
    for b in range(neighbours):
        for c in range(3):
            own_ref[b, c : c + 1, :] = own[c][b : b + 1, :]


def slots_body(owner_ref, master_ref, normal_ref, slot_ref, pay_ref, *, domains, cap):
    tiles = owner_ref.shape[0]
    slot_rows = pay_ref.shape[1]
    domain = lax.broadcasted_iota(jnp.int32, (domains, L), 0)
    tri = (lax.broadcasted_iota(jnp.int32, (L, L), 0) <= lax.broadcasted_iota(
        jnp.int32, (L, L), 1)).astype(F32).astype(BF16)
    seen = jnp.zeros((domains, 1), F32)
    for t in range(tiles):
        owner = owner_ref[t : t + 1, :]
        hit = domain == jnp.broadcast_to(owner, (domains, L))
        hits = jnp.where(hit, 1.0, 0.0)
        upto = jnp.dot(hits.astype(BF16), tri, preferred_element_type=F32) + seen
        rank = jnp.sum(jnp.where(hit, upto, 0.0), axis=0, keepdims=True) - 1.0
        slot_ref[t : t + 1, :] = owner * cap + rank.astype(jnp.int32)
        seen = seen + jnp.sum(hits, axis=1, keepdims=True)
    acc = None
    for t in range(0, tiles, 8):
        sl = slice(t, t + 8)
        values = [normal_ref[c, sl, :] for c in range(3)] + [master_ref[sl, :].astype(F32) + 1.0]
        got = scatter_tile(slot_ref[sl, :], values, slot_rows, 3)
        acc = got if acc is None else acc + got
    for c, value in enumerate(unstack(acc, 4, slot_rows, 3)):
        pay_ref[c] = value


def project_body(neighbours, u_ref, v_ref, shared_ref, int_ref, rec_ref, ext_ref, mass_ref,
                 accel_ref, rest_ref, slave_ref, slot_ref, normal_ref, x_ref, vn_ref, as_ref,
                 pay_ref):
    rows = u_ref.shape[1]
    slot_rows = pay_ref.shape[1]
    u, v, assembled = advance(
        [u_ref[c] for c in range(3)], [v_ref[c] for c in range(3)],
        [int_ref[c] for c in range(3)], by_part(rec_ref), shared_ref[...],
        [ext_ref[c] for c in range(3)], mass_ref[...], [accel_ref[c] for c in range(3)],
        rows, neighbours)
    for c in range(3):
        x_ref[c] = rest_ref[c] + u[c]
        vn_ref[c] = v[c]
        as_ref[c] = assembled[c]
    acc = None
    for t in range(0, slave_ref.shape[0], 8):
        sl = slice(t, t + 8)
        found = lookup(state_rows(x_ref, vn_ref, rows), slave_ref[sl, :])
        normal = [normal_ref[c, sl, :] for c in range(3)]
        along = sum(found[c] * normal[c] for c in range(3))
        speed = sum(found[3 + c] * normal[c] for c in range(3))
        got = scatter_tile(slot_ref[sl, :], [along, speed], slot_rows, 3)
        acc = got if acc is None else acc + got
    for c, value in enumerate(unstack(acc, 2, slot_rows, 3)):
        pay_ref[c] = value


def state_rows(x_ref, v_ref, rows):
    return table_rows(
        [lambda r, c=c: x_ref[c, r : r + 1, :] for c in range(3)]
        + [lambda r, c=c: v_ref[c, r : r + 1, :] for c in range(3)], rows)


def push_body(x_ref, v_ref, early_ref, late_ref, push_ref, force_ref, total):
    rows = x_ref.shape[1]
    total[...] = jnp.zeros_like(total)

    def step(i, carry):
        sl = pl.ds(pl.multiple_of(i * 8, 8), 8)
        coded = early_ref[3, sl, :]
        master = jnp.maximum(coded - 0.5, 0.0).astype(jnp.int32)
        normal = [early_ref[c, sl, :] for c in range(3)]
        found = lookup(state_rows(x_ref, v_ref, rows), master)
        gap = late_ref[0, sl, :] - sum(found[c] * normal[c] for c in range(3))
        closing = late_ref[1, sl, :] - sum(found[3 + c] * normal[c] for c in range(3))
        z = -gap / GAP_WIDTH
        soft = jnp.maximum(z, 0.0) + jnp.log1p(jnp.exp(-jnp.abs(z)))
        push = PENALTY * GAP_WIDTH * soft - CONTACT_DAMP * closing
        push = jnp.where(coded > 0.5, push, 0.0)
        push_ref[sl, :] = push
        total[...] += scatter_tile(master, [-push * normal[c] for c in range(3)], rows, 2)
        return carry

    lax.fori_loop(0, push_ref.shape[0] // 8, step, 0)
    for c, value in enumerate(unstack(total[...], 3, rows, 2)):
        force_ref[c] = value


def finish_body(x_ref, v_ref, as_ref, ext_ref, mass_ref, accel_ref, force_ref, push_ref, slot_ref,
                slave_ref, normal_ref, part_ref, nv_ref, sums_ref, vals, total):
    rows = x_ref.shape[1]
    push_rows = [[push_ref[r : r + 1, :]] for r in range(push_ref.shape[0])]
    acc = None
    for t in range(0, slave_ref.shape[0], 8):
        sl = slice(t, t + 8)
        push = lookup(push_rows, slot_ref[sl, :])[0]
        got = scatter_tile(slave_ref[sl, :], [push * normal_ref[c, sl, :] for c in range(3)],
                           rows, 2)
        acc = got if acc is None else acc + got
    slave_force = unstack(acc, 3, rows, 2)
    mass = mass_ref[...]
    x = [x_ref[c] for c in range(3)]
    net = []
    for c in range(3):
        force = force_ref[c] + slave_force[c]
        nv_ref[c] = v_ref[c] + TIME_STEP * force / mass
        net.append(ext_ref[c] - as_ref[c] + force - mass * accel_ref[c])
    turned = [x[1] * net[2] - x[2] * net[1], x[2] * net[0] - x[0] * net[2],
              x[0] * net[1] - x[1] * net[0]]
    for i, value in enumerate([mass] + [mass * x[c] for c in range(3)] + net + turned):
        vals[i] = value
    part_rows = sums_ref.shape[1]
    total[...] = jnp.zeros_like(total)

    def step(i, carry):
        sl = pl.ds(pl.multiple_of(i * 8, 8), 8)
        part = part_ref[sl, :]
        total[...] += scatter_tile(part, [vals[k, sl, :] for k in range(10)], part_rows, 3)
        return carry

    lax.fori_loop(0, rows // 8, step, 0)
    for k, value in enumerate(unstack(total[...], 10, part_rows, 3)):
        sums_ref[k] = value


def coords(index):
    return {"dom": index}


def greet(peers):
    barrier = pltpu.get_barrier_semaphore()
    for peer in peers:
        pl.semaphore_signal(barrier, inc=1, device_id=coords(peer),
                            device_id_type=pl.DeviceIdType.MESH)
    pl.semaphore_wait(barrier, len(peers))


def send(source, target, send_sem, recv_sem, peer):
    return pltpu.make_async_remote_copy(
        src_ref=source, dst_ref=target, send_sem=send_sem, recv_sem=recv_sem,
        device_id=coords(peer), device_id_type=pl.DeviceIdType.MESH)


def exchange_body(neighbours, own_ref, got_ref, send_sem, recv_sem):
    me = lax.axis_index("dom")
    peers = [me + (1 - 2 * ((me // 2**b) % 2)) * 2**b for b in range(neighbours)]
    greet(peers)
    copies = [send(own_ref.at[b], got_ref.at[b], send_sem.at[b], recv_sem.at[b], peers[b])
              for b in range(neighbours)]
    for copy in copies:
        copy.start()
    for copy in copies:
        copy.wait()


def swap_body(domains, in_ref, out_ref, send_sem, recv_sem, own_sem):
    me = lax.axis_index("dom")
    own = pltpu.make_async_copy(in_ref.at[me], out_ref.at[me], own_sem)
    own.start()
    barrier = pltpu.get_barrier_semaphore()

    def peer_at(apart):
        return (me + apart) % domains

    def hello(apart, carry):
        pl.semaphore_signal(barrier, inc=1, device_id=coords(peer_at(apart)),
                            device_id_type=pl.DeviceIdType.MESH)
        return carry

    lax.fori_loop(1, domains, hello, 0)
    pl.semaphore_wait(barrier, domains - 1)

    def copy(apart):
        peer = peer_at(apart)
        return send(in_ref.at[peer], out_ref.at[me], send_sem.at[apart], recv_sem.at[apart], peer)

    def begin(apart, carry):
        copy(apart).start()
        return carry

    def end(apart, carry):
        copy(apart).wait()
        return carry

    lax.fori_loop(1, domains, begin, 0)
    lax.fori_loop(1, domains, end, 0)
    own.wait()


def bit_groups(domains):
    bits = domains.bit_length() - 1
    groups, low = [], 0
    while low < bits:
        width = min(3, bits - low)
        if bits - low == 4:
            width = 2
        groups.append((low, width))
        low += width
    return groups


def total_body(domains, in_ref, out_ref, *scratch):
    groups = bit_groups(domains)
    held, partial, (send_sem, recv_sem, own_sem) = (
        scratch[:len(groups)], scratch[len(groups):2 * len(groups) - 1], scratch[-3:])
    me = lax.axis_index("dom")
    plans = []
    for low, width in groups:
        size = 2**width
        digit = (me // 2**low) % size
        base = me - digit * 2**low
        plans.append((digit, [base + ((digit + o) % size) * 2**low for o in range(1, size)]))
    greet([peer for _, peers in plans for peer in peers])
    source = in_ref
    place = 0
    for g, (digit, peers) in enumerate(plans):
        own = pltpu.make_async_copy(source, held[g].at[digit], own_sem.at[g])
        copies = [own]
        for i, peer in enumerate(peers):
            copies.append(send(source, held[g].at[digit], send_sem.at[place + i],
                               recv_sem.at[place + i], peer))
        place += len(peers)
        for copy in copies:
            copy.start()
        for copy in copies:
            copy.wait()
        value = held[g][0]
        for k in range(1, len(peers) + 1):
            value = value + held[g][k]
        if g + 1 < len(plans):
            partial[g][...] = value
            source = partial[g]
        else:
            out_ref[...] = value


VMEM = pl.BlockSpec(memory_space=pltpu.VMEM)
SMEM = pl.BlockSpec(memory_space=pltpu.SMEM)


def call(body, outs, scratch, specs, name, collective=None):
    return pl.pallas_call(
        body,
        out_shape=outs,
        in_specs=specs,
        out_specs=[VMEM] * len(outs),
        scratch_shapes=scratch,
        name=name,
        compiler_params=pltpu.CompilerParams(
            vmem_limit_bytes=48 * 2**20, collective_id=collective,
            has_side_effects=collective is not None),
    )


def cross_product(left, right):
    return jnp.stack([
        left[1] * right[2] - left[2] * right[1],
        left[2] * right[0] - left[0] * right[2],
        left[0] * right[1] - left[1] * right[0],
    ])


def f32(*shape):
    return jax.ShapeDtypeStruct(shape, F32)


def by_owner(payload, domains):
    count, slot_rows, _ = payload.shape
    each = slot_rows // domains
    return payload.reshape(count, domains, each, L).transpose(1, 0, 2, 3).reshape(
        domains, count * each, L)


def to_slots(payload, count):
    domains, each, _ = payload.shape
    each = each // count
    return payload.reshape(domains, count, each, L).transpose(1, 0, 2, 3).reshape(
        count, domains * each, L)


def swap(payload, domains, collective):
    return call(
        functools.partial(swap_body, domains), [f32(*payload.shape)],
        [pltpu.SemaphoreType.DMA((domains,))] * 2 + [pltpu.SemaphoreType.DMA], [VMEM], "swap",
        collective)(payload)[0]


def exchange(own):
    neighbours = own.shape[0]
    return call(
        functools.partial(exchange_body, neighbours), [f32(*own.shape)],
        [pltpu.SemaphoreType.DMA((neighbours,))] * 2, [VMEM], "exchange", 0)(own)[0]


def total_over(sums, domains):
    groups = bit_groups(domains)
    count = sum(2**width - 1 for _, width in groups)
    return call(
        functools.partial(total_body, domains), [f32(*sums.shape)],
        [pltpu.VMEM((2**width,) + sums.shape, F32) for _, width in groups]
        + [pltpu.VMEM(sums.shape, F32)] * (len(groups) - 1)
        + [pltpu.SemaphoreType.DMA((count,))] * 2 + [pltpu.SemaphoreType.DMA((len(groups),))],
        [VMEM], "total", 1)(sums)[0]


def per_device(rest_pos, displacement, velocity, ext_force, node_mass, body_accel, connectivity,
               elem_material, stiffness, shared_nodes, contact_slave, contact_owner,
               contact_master, contact_normal, part_of_node, part_mass, part_center,
               part_inertia):
    domains = lax.axis_size("dom")
    neighbours, shared_count = shared_nodes.shape[1:]
    nodes = displacement.shape[1]
    rows = nodes // L
    elems = connectivity.shape[1]
    blocks = elems // L
    contacts = contact_slave.shape[0]
    tiles = contacts // L
    cap = -(-(4 * contacts // domains) // L) * L
    slot_rows = domains * cap // L
    part_rows = -(-PARTS_SIZE // L)

    corners = (connectivity + jnp.arange(elems, dtype=jnp.int32)[None, :]) % nodes
    u = displacement.reshape(3, rows, L)
    v = velocity.reshape(3, rows, L)
    ext = ext_force.reshape(3, rows, L)
    rest = rest_pos.reshape(3, rows, L)
    mass = node_mass.reshape(rows, L)
    shared = jnp.concatenate(
        [shared_nodes[0], jnp.zeros((8 - neighbours, shared_count), jnp.int32)], 0)
    k_hi = lax.reduce_precision(stiffness, 8, 7)
    k_lo = stiffness - k_hi
    matrix = jnp.concatenate(
        [k_hi, k_hi, k_lo, jnp.zeros(stiffness.shape[:2] + (8,), F32)], 2).astype(BF16)
    materials = stiffness.shape[0]
    pick = (elem_material[:, None] == jnp.arange(materials, dtype=jnp.int32)[None]).astype(BF16)
    matrix = jnp.dot(pick, matrix.reshape(materials, -1), preferred_element_type=F32)
    matrix = matrix.astype(BF16).reshape(blocks, 24, 80)

    owner = contact_owner.reshape(tiles, L)
    master = contact_master.reshape(tiles, L)
    slave = contact_slave.reshape(tiles, L)
    normal = contact_normal.reshape(3, tiles, L)
    slot, early = call(
        functools.partial(slots_body, domains=domains, cap=cap),
        [jax.ShapeDtypeStruct((tiles, L), jnp.int32), f32(4, slot_rows, L)], [],
        [VMEM] * 3, "slots")(owner, master, normal)
    early = to_slots(swap(by_owner(early, domains), domains, 2), 4)

    node_shape = f32(3, rows, L)
    own_shape = f32(neighbours, 8, L)
    scratch = [pltpu.VMEM((3, rows, L), F32), pltpu.VMEM((6 * rows, L), F32)]
    received = internal = None
    for cycle in range(CYCLES):
        if cycle == 0:
            internal, own = call(
                functools.partial(elem_body, True, neighbours), [node_shape, own_shape], scratch,
                [VMEM] * 5, "elements")(u, v, corners, shared, matrix)
        else:
            internal, own, u, v = call(
                functools.partial(elem_body, False, neighbours),
                [node_shape, own_shape, node_shape, node_shape], scratch,
                [VMEM] * 9 + [SMEM], "elements")(
                    u, v, corners, shared, matrix, internal, received, ext, mass, body_accel)
        received = exchange(own)

    x, v, assembled, late = call(
        functools.partial(project_body, neighbours),
        [node_shape, node_shape, node_shape, f32(2, slot_rows, L)], [],
        [VMEM] * 7 + [SMEM] + [VMEM] * 4, "project")(
            u, v, shared, internal, received, ext, mass, body_accel, rest, slave, slot, normal)
    late = to_slots(swap(by_owner(late, domains), domains, 3), 2)
    push, force = call(
        push_body, [f32(slot_rows, L), node_shape], [pltpu.VMEM((6 * rows, L), F32)],
        [VMEM] * 4, "push")(x, v, early, late)
    push = to_slots(swap(by_owner(push[None], domains), domains, 4), 1)[0]
    nodal_velocity, sums = call(
        finish_body, [node_shape, f32(10, part_rows, L)],
        [pltpu.VMEM((10, rows, L), F32), pltpu.VMEM((30 * part_rows, L), F32)],
        [VMEM] * 5 + [SMEM] + [VMEM] * 6, "finish")(
            x, v, assembled, ext, mass, body_accel, force, push, slot, slave, normal,
            part_of_node.reshape(rows, L))
    totals = total_over(sums, domains).reshape(10, part_rows * L)[:, :PARTS_SIZE]
    mass_total = part_mass + totals[0]
    centre = (part_mass[None] * part_center + totals[1:4]) / mass_total[None]
    force_sum = totals[4:7]
    torque = totals[7:10] - cross_product(centre, force_sum)
    part_motion = jnp.concatenate([force_sum / mass_total[None], torque / part_inertia], 0)
    return nodal_velocity.reshape(3, nodes), part_motion


def solution(mesh):
    placed = (
        P(None, "dom"), P(None, "dom"), P(None, "dom"), P(None, "dom"), P("dom"), P(),
        P(None, "dom"), P("dom"), P(), P("dom", None, None), P("dom"), P("dom", None), P("dom"),
        P(None, "dom"), P("dom"), P(), P(), P(),
    )
    return jax.shard_map(
        per_device, mesh=mesh, in_specs=placed, out_specs=(P(None, "dom"), P()), check_vma=False
    )
```

```python
import functools

import jax
import jax.numpy as jnp
from jax import lax
from jax.experimental import pallas as pl
from jax.experimental.pallas import tpu as pltpu
from jax.sharding import PartitionSpec as P

CYCLES = 3
PARTS_SIZE = 400
TIME_STEP = 0.1
DAMP_RATIO = 0.05
PENALTY = 2.0
GAP_WIDTH = 0.5
CONTACT_DAMP = 0.2
L = 128
GROUP = 4
F32 = jnp.float32
BF16 = jnp.bfloat16
NT = (((1,), (1,)), ((), ()))


def lookup(tables, index):
    high = index >> 7
    low = index & 127
    found = [None] * len(tables[0])
    for r, rows in enumerate(tables):
        hit = high == r
        for c, row in enumerate(rows):
            got = jnp.take_along_axis(
                jnp.broadcast_to(row, index.shape), low, axis=1, mode="promise_in_bounds"
            )
            found[c] = got if found[c] is None else jnp.where(hit, got, found[c])
    return found


def table_rows(refs, rows):
    return [[ref(r) for ref in refs] for r in range(rows)]


def scatter_tile(index, values, rows, pieces, live=None):
    high = (index >> 7).astype(F32)
    low = (index & 127).astype(F32)
    sublane = lax.broadcasted_iota(jnp.int32, (max(rows, 16), L), 0).astype(F32).astype(BF16)
    place = lax.broadcasted_iota(jnp.int32, (L, L), 0).astype(F32).astype(BF16)
    one, zero = jnp.ones((), BF16), jnp.zeros((), BF16)
    parts = []
    for value in values:
        value = jnp.concatenate(value, 0) if isinstance(value, list) else value
        for p in range(pieces):
            piece = value.astype(BF16).astype(F32) if p + 1 < pieces else value
            parts.append(piece)
            value = value - piece
    left, right = [], []

    def spread(value, s, count):
        row = jnp.broadcast_to(value[s : s + 1, :], (16, L)).astype(BF16)
        return jnp.concatenate([row] * (count // 16), 0) if count > 16 else row

    for s in range(live or index.shape[0]):
        mine = sublane == spread(high, s, sublane.shape[0])
        left.append(jnp.concatenate(
            [jnp.where(mine, spread(part, s, sublane.shape[0]), zero) for part in parts], 0))
        right.append(jnp.where(place == spread(low, s, L), one, zero))
    return lax.dot_general(
        jnp.concatenate(left, 1), jnp.concatenate(right, 1), NT, preferred_element_type=F32
    )


def unstack(total, count, rows, pieces):
    out = []
    step = max(rows, 16)
    for c in range(count):
        base = c * pieces * step
        value = total[base : base + rows]
        for p in range(1, pieces):
            value = value + total[base + p * step : base + p * step + rows]
        out.append(value)
    return out


def advance(u, v, internal, received, shared, ext, mass, accel, rows, neighbours):
    added = unstack(scatter_tile(shared, received, rows, 3, neighbours), 3, rows, 3)
    assembled = [internal[c] + added[c] for c in range(3)]
    v = [v[c] + TIME_STEP * ((ext[c] - assembled[c]) / mass - accel[c]) for c in range(3)]
    u = [u[c] + TIME_STEP * v[c] for c in range(3)]
    return u, v, assembled


def by_part(rec_ref):
    return [[rec_ref[b, c : c + 1, :] for b in range(rec_ref.shape[0])] for c in range(3)]


def elem_body(first, neighbours, *refs):
    if first:
        u_ref, v_ref, corner_ref, shared_ref, matrix_ref, out_ref, own_ref, field, total = refs
        u = [u_ref[c] for c in range(3)]
        v = [v_ref[c] for c in range(3)]
    else:
        (u_ref, v_ref, corner_ref, shared_ref, matrix_ref, int_ref, rec_ref, ext_ref, mass_ref,
         accel_ref, out_ref, own_ref, un_ref, vn_ref, field, total) = refs
        rows = u_ref.shape[1]
        u, v, _ = advance(
            [u_ref[c] for c in range(3)], [v_ref[c] for c in range(3)],
            [int_ref[c] for c in range(3)], by_part(rec_ref), shared_ref[...],
            [ext_ref[c] for c in range(3)], mass_ref[...], [accel_ref[c] for c in range(3)],
            rows, neighbours)
        for c in range(3):
            un_ref[c] = u[c]
            vn_ref[c] = v[c]
    rows = u_ref.shape[1]
    for c in range(3):
        field[c] = u[c] + DAMP_RATIO * v[c]
    total[...] = jnp.zeros_like(total)
    blocks = corner_ref.shape[1] // L

    def corner_index(b):
        return corner_ref[:, pl.ds(pl.multiple_of(b * L, L), L)]

    def forces(b):
        found = lookup(
            table_rows([lambda r, c=c: field[c, r : r + 1, :] for c in range(3)], rows),
            corner_index(b))
        g = jnp.concatenate(found, 0)
        g_hi = g.astype(BF16).astype(F32)
        rhs = jnp.concatenate([g_hi, g - g_hi, g_hi, jnp.zeros((8, L), F32)], 0).astype(BF16)
        h = jnp.dot(matrix_ref[b], rhs, preferred_element_type=F32)
        return h[0:8], h[8:16], h[16:24]

    def group(i):
        each = [forces(i * GROUP + k) for k in range(GROUP)]
        return tuple(jnp.concatenate([h[c] for h in each], 0) for c in range(3))

    def add_group(i, held):
        index = jnp.concatenate([corner_index(i * GROUP + k) for k in range(GROUP)], 0)
        total[...] += scatter_tile(index, list(held), rows, 2)

    def step(i, held):
        coming = group(i)
        add_group(i - 1, held)
        return coming

    groups = blocks // GROUP
    add_group(groups - 1, lax.fori_loop(1, groups, step, group(0)))
    internal = unstack(total[...], 3, rows, 2)
    for c in range(3):
        out_ref[c] = internal[c]
        field[c] = internal[c]
    own = lookup(
        table_rows([lambda r, c=c: field[c, r : r + 1, :] for c in range(3)], rows),
        shared_ref[...])
    for b in range(neighbours):
        for c in range(3):
            own_ref[b, c : c + 1, :] = own[c][b : b + 1, :]


def slots_body(owner_ref, master_ref, normal_ref, slot_ref, pay_ref, *, domains, cap):
    tiles = owner_ref.shape[0]
    slot_rows = pay_ref.shape[1]
    domain = lax.broadcasted_iota(jnp.int32, (domains, L), 0)
    tri = (lax.broadcasted_iota(jnp.int32, (L, L), 0) <= lax.broadcasted_iota(
        jnp.int32, (L, L), 1)).astype(F32).astype(BF16)
    seen = jnp.zeros((domains, 1), F32)
    for t in range(tiles):
        owner = owner_ref[t : t + 1, :]
        hit = domain == jnp.broadcast_to(owner, (domains, L))
        hits = jnp.where(hit, 1.0, 0.0)
        upto = jnp.dot(hits.astype(BF16), tri, preferred_element_type=F32) + seen
        rank = jnp.sum(jnp.where(hit, upto, 0.0), axis=0, keepdims=True) - 1.0
        slot_ref[t : t + 1, :] = owner * cap + rank.astype(jnp.int32)
        seen = seen + jnp.sum(hits, axis=1, keepdims=True)
    acc = None
    for t in range(0, tiles, 8):
        sl = slice(t, t + 8)
        values = [normal_ref[c, sl, :] for c in range(3)] + [master_ref[sl, :].astype(F32) + 1.0]
        got = scatter_tile(slot_ref[sl, :], values, slot_rows, 3)
        acc = got if acc is None else acc + got
    for c, value in enumerate(unstack(acc, 4, slot_rows, 3)):
        pay_ref[c] = value


def project_body(neighbours, u_ref, v_ref, shared_ref, int_ref, rec_ref, ext_ref, mass_ref,
                 accel_ref, rest_ref, slave_ref, slot_ref, normal_ref, x_ref, vn_ref, as_ref,
                 pay_ref):
    rows = u_ref.shape[1]
    slot_rows = pay_ref.shape[1]
    u, v, assembled = advance(
        [u_ref[c] for c in range(3)], [v_ref[c] for c in range(3)],
        [int_ref[c] for c in range(3)], by_part(rec_ref), shared_ref[...],
        [ext_ref[c] for c in range(3)], mass_ref[...], [accel_ref[c] for c in range(3)],
        rows, neighbours)
    for c in range(3):
        x_ref[c] = rest_ref[c] + u[c]
        vn_ref[c] = v[c]
        as_ref[c] = assembled[c]
    acc = None
    for t in range(0, slave_ref.shape[0], 8):
        sl = slice(t, t + 8)
        found = lookup(state_rows(x_ref, vn_ref, rows), slave_ref[sl, :])
        normal = [normal_ref[c, sl, :] for c in range(3)]
        along = sum(found[c] * normal[c] for c in range(3))
        speed = sum(found[3 + c] * normal[c] for c in range(3))
        got = scatter_tile(slot_ref[sl, :], [along, speed], slot_rows, 3)
        acc = got if acc is None else acc + got
    for c, value in enumerate(unstack(acc, 2, slot_rows, 3)):
        pay_ref[c] = value


def state_rows(x_ref, v_ref, rows):
    return table_rows(
        [lambda r, c=c: x_ref[c, r : r + 1, :] for c in range(3)]
        + [lambda r, c=c: v_ref[c, r : r + 1, :] for c in range(3)], rows)


def push_body(x_ref, v_ref, sent_ref, push_ref, force_ref, total):
    rows = x_ref.shape[1]
    total[...] = jnp.zeros_like(total)

    def step(i, carry):
        sl = pl.ds(pl.multiple_of(i * 8, 8), 8)
        coded = sent_ref[3, sl, :]
        master = jnp.maximum(coded - 0.5, 0.0).astype(jnp.int32)
        normal = [sent_ref[c, sl, :] for c in range(3)]
        found = lookup(state_rows(x_ref, v_ref, rows), master)
        gap = sent_ref[4, sl, :] - sum(found[c] * normal[c] for c in range(3))
        closing = sent_ref[5, sl, :] - sum(found[3 + c] * normal[c] for c in range(3))
        z = -gap / GAP_WIDTH
        soft = jnp.maximum(z, 0.0) + jnp.log1p(jnp.exp(-jnp.abs(z)))
        push = PENALTY * GAP_WIDTH * soft - CONTACT_DAMP * closing
        push = jnp.where(coded > 0.5, push, 0.0)
        push_ref[sl, :] = push
        total[...] += scatter_tile(master, [-push * normal[c] for c in range(3)], rows, 2)
        return carry

    lax.fori_loop(0, push_ref.shape[0] // 8, step, 0)
    for c, value in enumerate(unstack(total[...], 3, rows, 2)):
        force_ref[c] = value


def finish_body(x_ref, v_ref, as_ref, ext_ref, mass_ref, accel_ref, force_ref, push_ref, slot_ref,
                slave_ref, normal_ref, part_ref, nv_ref, sums_ref, vals, total):
    rows = x_ref.shape[1]
    push_rows = [[push_ref[r : r + 1, :]] for r in range(push_ref.shape[0])]
    acc = None
    for t in range(0, slave_ref.shape[0], 8):
        sl = slice(t, t + 8)
        push = lookup(push_rows, slot_ref[sl, :])[0]
        got = scatter_tile(slave_ref[sl, :], [push * normal_ref[c, sl, :] for c in range(3)],
                           rows, 2)
        acc = got if acc is None else acc + got
    slave_force = unstack(acc, 3, rows, 2)
    mass = mass_ref[...]
    x = [x_ref[c] for c in range(3)]
    net = []
    for c in range(3):
        force = force_ref[c] + slave_force[c]
        nv_ref[c] = v_ref[c] + TIME_STEP * force / mass
        net.append(ext_ref[c] - as_ref[c] + force - mass * accel_ref[c])
    turned = [x[1] * net[2] - x[2] * net[1], x[2] * net[0] - x[0] * net[2],
              x[0] * net[1] - x[1] * net[0]]
    for i, value in enumerate([mass] + [mass * x[c] for c in range(3)] + net + turned):
        vals[i] = value
    part_rows = sums_ref.shape[1]
    total[...] = jnp.zeros_like(total)

    def step(i, carry):
        sl = pl.ds(pl.multiple_of(i * 8, 8), 8)
        part = part_ref[sl, :]
        total[...] += scatter_tile(part, [vals[k, sl, :] for k in range(10)], part_rows, 3)
        return carry

    lax.fori_loop(0, rows // 8, step, 0)
    for k, value in enumerate(unstack(total[...], 10, part_rows, 3)):
        sums_ref[k] = value


def coords(index):
    return {"dom": index}


def greet(peers):
    barrier = pltpu.get_barrier_semaphore()
    for peer in peers:
        pl.semaphore_signal(barrier, inc=1, device_id=coords(peer),
                            device_id_type=pl.DeviceIdType.MESH)
    pl.semaphore_wait(barrier, len(peers))


def send(source, target, send_sem, recv_sem, peer):
    return pltpu.make_async_remote_copy(
        src_ref=source, dst_ref=target, send_sem=send_sem, recv_sem=recv_sem,
        device_id=coords(peer), device_id_type=pl.DeviceIdType.MESH)


def exchange_body(neighbours, own_ref, got_ref, send_sem, recv_sem):
    me = lax.axis_index("dom")
    peers = [me + (1 - 2 * ((me // 2**b) % 2)) * 2**b for b in range(neighbours)]
    greet(peers)
    copies = [send(own_ref.at[b], got_ref.at[b], send_sem.at[b], recv_sem.at[b], peers[b])
              for b in range(neighbours)]
    for copy in copies:
        copy.start()
    for copy in copies:
        copy.wait()


def swap_body(domains, in_ref, out_ref, send_sem, recv_sem, own_sem):
    me = lax.axis_index("dom")
    own = pltpu.make_async_copy(in_ref.at[me], out_ref.at[me], own_sem)
    own.start()
    peers = [(me + apart) % domains for apart in range(1, domains)]
    greet(peers)
    copies = [send(in_ref.at[peer], out_ref.at[me], send_sem.at[i], recv_sem.at[i], peer)
              for i, peer in enumerate(peers)]
    for copy in copies:
        copy.start()
    for copy in copies:
        copy.wait()
    own.wait()


def bit_groups(domains):
    bits = domains.bit_length() - 1
    groups, low = [], 0
    while low < bits:
        width = min(3, bits - low)
        if bits - low == 4:
            width = 2
        groups.append((low, width))
        low += width
    return groups


def total_body(domains, in_ref, out_ref, *scratch):
    groups = bit_groups(domains)
    held, partial, (send_sem, recv_sem, own_sem) = (
        scratch[:len(groups)], scratch[len(groups):2 * len(groups) - 1], scratch[-3:])
    me = lax.axis_index("dom")
    plans = []
    for low, width in groups:
        size = 2**width
        digit = (me // 2**low) % size
        base = me - digit * 2**low
        plans.append((digit, [base + ((digit + o) % size) * 2**low for o in range(1, size)]))
    greet([peer for _, peers in plans for peer in peers])
    source = in_ref
    place = 0
    for g, (digit, peers) in enumerate(plans):
        own = pltpu.make_async_copy(source, held[g].at[digit], own_sem.at[g])
        copies = [own]
        for i, peer in enumerate(peers):
            copies.append(send(source, held[g].at[digit], send_sem.at[place + i],
                               recv_sem.at[place + i], peer))
        place += len(peers)
        for copy in copies:
            copy.start()
        for copy in copies:
            copy.wait()
        value = held[g][0]
        for k in range(1, len(peers) + 1):
            value = value + held[g][k]
        if g + 1 < len(plans):
            partial[g][...] = value
            source = partial[g]
        else:
            out_ref[...] = value


VMEM = pl.BlockSpec(memory_space=pltpu.VMEM)
SMEM = pl.BlockSpec(memory_space=pltpu.SMEM)


def call(body, outs, scratch, specs, name, collective=None):
    return pl.pallas_call(
        body,
        out_shape=outs,
        in_specs=specs,
        out_specs=[VMEM] * len(outs),
        scratch_shapes=scratch,
        name=name,
        compiler_params=pltpu.CompilerParams(
            vmem_limit_bytes=48 * 2**20, collective_id=collective,
            has_side_effects=collective is not None),
    )


def cross_product(left, right):
    return jnp.stack([
        left[1] * right[2] - left[2] * right[1],
        left[2] * right[0] - left[0] * right[2],
        left[0] * right[1] - left[1] * right[0],
    ])


def f32(*shape):
    return jax.ShapeDtypeStruct(shape, F32)


def by_owner(payload, domains):
    count, slot_rows, _ = payload.shape
    each = slot_rows // domains
    return payload.reshape(count, domains, each, L).transpose(1, 0, 2, 3).reshape(
        domains, count * each, L)


def to_slots(payload, count):
    domains, each, _ = payload.shape
    each = each // count
    return payload.reshape(domains, count, each, L).transpose(1, 0, 2, 3).reshape(
        count, domains * each, L)


def swap(payload, domains, collective):
    return call(
        functools.partial(swap_body, domains), [f32(*payload.shape)],
        [pltpu.SemaphoreType.DMA((domains,))] * 2 + [pltpu.SemaphoreType.DMA], [VMEM], "swap",
        collective)(payload)[0]


def exchange(own):
    neighbours = own.shape[0]
    return call(
        functools.partial(exchange_body, neighbours), [f32(*own.shape)],
        [pltpu.SemaphoreType.DMA((neighbours,))] * 2, [VMEM], "exchange", 0)(own)[0]


def total_over(sums, domains):
    groups = bit_groups(domains)
    count = sum(2**width - 1 for _, width in groups)
    return call(
        functools.partial(total_body, domains), [f32(*sums.shape)],
        [pltpu.VMEM((2**width,) + sums.shape, F32) for _, width in groups]
        + [pltpu.VMEM(sums.shape, F32)] * (len(groups) - 1)
        + [pltpu.SemaphoreType.DMA((count,))] * 2 + [pltpu.SemaphoreType.DMA((len(groups),))],
        [VMEM], "total", 1)(sums)[0]


def per_device(rest_pos, displacement, velocity, ext_force, node_mass, body_accel, connectivity,
               elem_material, stiffness, shared_nodes, contact_slave, contact_owner,
               contact_master, contact_normal, part_of_node, part_mass, part_center,
               part_inertia):
    domains = lax.axis_size("dom")
    neighbours, shared_count = shared_nodes.shape[1:]
    nodes = displacement.shape[1]
    rows = nodes // L
    elems = connectivity.shape[1]
    blocks = elems // L
    contacts = contact_slave.shape[0]
    tiles = contacts // L
    cap = -(-(4 * contacts // domains) // L) * L
    slot_rows = domains * cap // L
    part_rows = -(-PARTS_SIZE // L)

    corners = (connectivity + jnp.arange(elems, dtype=jnp.int32)[None, :]) % nodes
    u = displacement.reshape(3, rows, L)
    v = velocity.reshape(3, rows, L)
    ext = ext_force.reshape(3, rows, L)
    rest = rest_pos.reshape(3, rows, L)
    mass = node_mass.reshape(rows, L)
    shared = jnp.concatenate(
        [shared_nodes[0], jnp.zeros((8 - neighbours, shared_count), jnp.int32)], 0)
    k_hi = lax.reduce_precision(stiffness, 8, 7)
    k_lo = stiffness - k_hi
    matrix = jnp.concatenate(
        [k_hi, k_hi, k_lo, jnp.zeros(stiffness.shape[:2] + (8,), F32)], 2).astype(BF16)
    materials = stiffness.shape[0]
    pick = (elem_material[:, None] == jnp.arange(materials, dtype=jnp.int32)[None]).astype(BF16)
    matrix = jnp.dot(pick, matrix.reshape(materials, -1), preferred_element_type=F32)
    matrix = matrix.astype(BF16).reshape(blocks, 24, 80)

    owner = contact_owner.reshape(tiles, L)
    master = contact_master.reshape(tiles, L)
    slave = contact_slave.reshape(tiles, L)
    normal = contact_normal.reshape(3, tiles, L)
    slot, early = call(
        functools.partial(slots_body, domains=domains, cap=cap),
        [jax.ShapeDtypeStruct((tiles, L), jnp.int32), f32(4, slot_rows, L)], [],
        [VMEM] * 3, "slots")(owner, master, normal)

    node_shape = f32(3, rows, L)
    own_shape = f32(neighbours, 8, L)
    scratch = [pltpu.VMEM((3, rows, L), F32), pltpu.VMEM((6 * rows, L), F32)]
    received = internal = None
    for cycle in range(CYCLES):
        if cycle == 0:
            internal, own = call(
                functools.partial(elem_body, True, neighbours), [node_shape, own_shape], scratch,
                [VMEM] * 5, "elements")(u, v, corners, shared, matrix)
        else:
            internal, own, u, v = call(
                functools.partial(elem_body, False, neighbours),
                [node_shape, own_shape, node_shape, node_shape], scratch,
                [VMEM] * 9 + [SMEM], "elements")(
                    u, v, corners, shared, matrix, internal, received, ext, mass, body_accel)
        received = exchange(own)

    x, v, assembled, late = call(
        functools.partial(project_body, neighbours),
        [node_shape, node_shape, node_shape, f32(2, slot_rows, L)], [],
        [VMEM] * 7 + [SMEM] + [VMEM] * 4, "project")(
            u, v, shared, internal, received, ext, mass, body_accel, rest, slave, slot, normal)
    sent = jnp.concatenate([early, late], 0)
    sent = to_slots(swap(by_owner(sent, domains), domains, 3), 6)
    push, force = call(
        push_body, [f32(slot_rows, L), node_shape], [pltpu.VMEM((6 * rows, L), F32)],
        [VMEM] * 3, "push")(x, v, sent)
    push = to_slots(swap(by_owner(push[None], domains), domains, 4), 1)[0]
    nodal_velocity, sums = call(
        finish_body, [node_shape, f32(10, part_rows, L)],
        [pltpu.VMEM((10, rows, L), F32), pltpu.VMEM((30 * max(part_rows, 16), L), F32)],
        [VMEM] * 5 + [SMEM] + [VMEM] * 6, "finish")(
            x, v, assembled, ext, mass, body_accel, force, push, slot, slave, normal,
            part_of_node.reshape(rows, L))
    totals = total_over(sums, domains).reshape(10, part_rows * L)[:, :PARTS_SIZE]
    mass_total = part_mass + totals[0]
    centre = (part_mass[None] * part_center + totals[1:4]) / mass_total[None]
    force_sum = totals[4:7]
    torque = totals[7:10] - cross_product(centre, force_sum)
    part_motion = jnp.concatenate([force_sum / mass_total[None], torque / part_inertia], 0)
    return nodal_velocity.reshape(3, nodes), part_motion


def solution(mesh):
    placed = (
        P(None, "dom"), P(None, "dom"), P(None, "dom"), P(None, "dom"), P("dom"), P(),
        P(None, "dom"), P("dom"), P(), P("dom", None, None), P("dom"), P("dom", None), P("dom"),
        P(None, "dom"), P("dom"), P(), P(), P(),
    )
    return jax.shard_map(
        per_device, mesh=mesh, in_specs=placed, out_specs=(P(None, "dom"), P()), check_vma=False
    )
```

```python
import functools

import jax
import jax.numpy as jnp
from jax import lax
from jax.experimental import pallas as pl
from jax.experimental.pallas import tpu as pltpu
from jax.sharding import PartitionSpec as P

CYCLES = 3
PARTS_SIZE = 400
TIME_STEP = 0.1
DAMP_RATIO = 0.05
PENALTY = 2.0
GAP_WIDTH = 0.5
CONTACT_DAMP = 0.2
L = 128
GROUP = 4
F32 = jnp.float32
BF16 = jnp.bfloat16
NT = (((1,), (1,)), ((), ()))


def lookup(tables, index):
    high = index >> 7
    low = index & 127
    found = [None] * len(tables[0])
    for r, rows in enumerate(tables):
        hit = high == r
        for c, row in enumerate(rows):
            got = jnp.take_along_axis(
                jnp.broadcast_to(row, index.shape), low, axis=1, mode="promise_in_bounds"
            )
            found[c] = got if found[c] is None else jnp.where(hit, got, found[c])
    return found


def table_rows(refs, rows):
    return [[ref(r) for ref in refs] for r in range(rows)]


def scatter_tile(index, values, rows, pieces, live=None):
    high = (index >> 7).astype(F32)
    low = (index & 127).astype(F32)
    sublane = lax.broadcasted_iota(jnp.int32, (max(rows, 16), L), 0).astype(F32).astype(BF16)
    place = lax.broadcasted_iota(jnp.int32, (L, L), 0).astype(F32).astype(BF16)
    one, zero = jnp.ones((), BF16), jnp.zeros((), BF16)
    parts = []
    for value in values:
        value = jnp.concatenate(value, 0) if isinstance(value, list) else value
        for p in range(pieces):
            piece = value.astype(BF16).astype(F32) if p + 1 < pieces else value
            parts.append(piece)
            value = value - piece
    left, right = [], []

    def spread(value, s, count):
        row = jnp.broadcast_to(value[s : s + 1, :], (16, L)).astype(BF16)
        return jnp.concatenate([row] * (count // 16), 0) if count > 16 else row

    for s in range(live or index.shape[0]):
        mine = sublane == spread(high, s, sublane.shape[0])
        left.append(jnp.concatenate(
            [jnp.where(mine, spread(part, s, sublane.shape[0]), zero) for part in parts], 0))
        right.append(jnp.where(place == spread(low, s, L), one, zero))
    return lax.dot_general(
        jnp.concatenate(left, 1), jnp.concatenate(right, 1), NT, preferred_element_type=F32
    )


def unstack(total, count, rows, pieces):
    out = []
    step = max(rows, 16)
    for c in range(count):
        base = c * pieces * step
        value = total[base : base + rows]
        for p in range(1, pieces):
            value = value + total[base + p * step : base + p * step + rows]
        out.append(value)
    return out


def advance(u, v, internal, received, shared, ext, mass, accel, rows, neighbours):
    added = unstack(scatter_tile(shared, received, rows, 3, neighbours), 3, rows, 3)
    assembled = [internal[c] + added[c] for c in range(3)]
    v = [v[c] + TIME_STEP * ((ext[c] - assembled[c]) / mass - accel[c]) for c in range(3)]
    u = [u[c] + TIME_STEP * v[c] for c in range(3)]
    return u, v, assembled


def by_part(rec_ref):
    return [[rec_ref[b, c : c + 1, :] for b in range(rec_ref.shape[0])] for c in range(3)]


def elem_body(first, neighbours, *refs):
    if first:
        u_ref, v_ref, corner_ref, shared_ref, matrix_ref, out_ref, own_ref, field, total = refs
        u = [u_ref[c] for c in range(3)]
        v = [v_ref[c] for c in range(3)]
    else:
        (u_ref, v_ref, corner_ref, shared_ref, matrix_ref, int_ref, rec_ref, ext_ref, mass_ref,
         accel_ref, out_ref, own_ref, un_ref, vn_ref, field, total) = refs
        rows = u_ref.shape[1]
        u, v, _ = advance(
            [u_ref[c] for c in range(3)], [v_ref[c] for c in range(3)],
            [int_ref[c] for c in range(3)], by_part(rec_ref), shared_ref[...],
            [ext_ref[c] for c in range(3)], mass_ref[...], [accel_ref[c] for c in range(3)],
            rows, neighbours)
        for c in range(3):
            un_ref[c] = u[c]
            vn_ref[c] = v[c]
    rows = u_ref.shape[1]
    for c in range(3):
        field[c] = u[c] + DAMP_RATIO * v[c]
    total[...] = jnp.zeros_like(total)
    blocks = corner_ref.shape[1] // L

    def corner_index(b):
        return corner_ref[:, pl.ds(pl.multiple_of(b * L, L), L)]

    def forces(b):
        found = lookup(
            table_rows([lambda r, c=c: field[c, r : r + 1, :] for c in range(3)], rows),
            corner_index(b))
        g = jnp.concatenate(found, 0)
        g_hi = g.astype(BF16).astype(F32)
        rhs = jnp.concatenate([g_hi, g - g_hi, g_hi, jnp.zeros((8, L), F32)], 0).astype(BF16)
        h = jnp.dot(matrix_ref[b], rhs, preferred_element_type=F32)
        return h[0:8], h[8:16], h[16:24]

    def group(i):
        each = [forces(i * GROUP + k) for k in range(GROUP)]
        return tuple(jnp.concatenate([h[c] for h in each], 0) for c in range(3))

    def add_group(i, held):
        index = jnp.concatenate([corner_index(i * GROUP + k) for k in range(GROUP)], 0)
        total[...] += scatter_tile(index, list(held), rows, 2)

    def step(i, held):
        coming = group(i)
        add_group(i - 1, held)
        return coming

    groups = blocks // GROUP
    add_group(groups - 1, lax.fori_loop(1, groups, step, group(0)))
    internal = unstack(total[...], 3, rows, 2)
    for c in range(3):
        out_ref[c] = internal[c]
        field[c] = internal[c]
    own = lookup(
        table_rows([lambda r, c=c: field[c, r : r + 1, :] for c in range(3)], rows),
        shared_ref[...])
    for b in range(neighbours):
        for c in range(3):
            own_ref[b, c : c + 1, :] = own[c][b : b + 1, :]


def slots_body(owner_ref, master_ref, normal_ref, slot_ref, pay_ref, *, domains, cap):
    tiles = owner_ref.shape[0]
    slot_rows = pay_ref.shape[1]
    domain = lax.broadcasted_iota(jnp.int32, (domains, L), 0)
    tri = (lax.broadcasted_iota(jnp.int32, (L, L), 0) <= lax.broadcasted_iota(
        jnp.int32, (L, L), 1)).astype(F32).astype(BF16)
    seen = jnp.zeros((domains, 1), F32)
    for t in range(tiles):
        owner = owner_ref[t : t + 1, :]
        hit = domain == jnp.broadcast_to(owner, (domains, L))
        hits = jnp.where(hit, 1.0, 0.0)
        upto = jnp.dot(hits.astype(BF16), tri, preferred_element_type=F32) + seen
        rank = jnp.sum(jnp.where(hit, upto, 0.0), axis=0, keepdims=True) - 1.0
        slot_ref[t : t + 1, :] = owner * cap + rank.astype(jnp.int32)
        seen = seen + jnp.sum(hits, axis=1, keepdims=True)
    acc = None
    for t in range(0, tiles, 8):
        sl = slice(t, t + 8)
        values = [normal_ref[c, sl, :] for c in range(3)] + [master_ref[sl, :].astype(F32) + 1.0]
        got = scatter_tile(slot_ref[sl, :], values, slot_rows, 3)
        acc = got if acc is None else acc + got
    for c, value in enumerate(unstack(acc, 4, slot_rows, 3)):
        pay_ref[c] = value


def project_body(neighbours, u_ref, v_ref, shared_ref, int_ref, rec_ref, ext_ref, mass_ref,
                 accel_ref, rest_ref, slave_ref, slot_ref, normal_ref, x_ref, vn_ref, as_ref,
                 pay_ref):
    rows = u_ref.shape[1]
    slot_rows = pay_ref.shape[1]
    u, v, assembled = advance(
        [u_ref[c] for c in range(3)], [v_ref[c] for c in range(3)],
        [int_ref[c] for c in range(3)], by_part(rec_ref), shared_ref[...],
        [ext_ref[c] for c in range(3)], mass_ref[...], [accel_ref[c] for c in range(3)],
        rows, neighbours)
    for c in range(3):
        x_ref[c] = rest_ref[c] + u[c]
        vn_ref[c] = v[c]
        as_ref[c] = assembled[c]
    acc = None
    for t in range(0, slave_ref.shape[0], 8):
        sl = slice(t, t + 8)
        found = lookup(state_rows(x_ref, vn_ref, rows), slave_ref[sl, :])
        normal = [normal_ref[c, sl, :] for c in range(3)]
        along = sum(found[c] * normal[c] for c in range(3))
        speed = sum(found[3 + c] * normal[c] for c in range(3))
        got = scatter_tile(slot_ref[sl, :], [along, speed], slot_rows, 3)
        acc = got if acc is None else acc + got
    for c, value in enumerate(unstack(acc, 2, slot_rows, 3)):
        pay_ref[c] = value


def state_rows(x_ref, v_ref, rows):
    return table_rows(
        [lambda r, c=c: x_ref[c, r : r + 1, :] for c in range(3)]
        + [lambda r, c=c: v_ref[c, r : r + 1, :] for c in range(3)], rows)


def push_body(x_ref, v_ref, sent_ref, push_ref, force_ref, total):
    rows = x_ref.shape[1]
    total[...] = jnp.zeros_like(total)

    def step(i, carry):
        sl = pl.ds(pl.multiple_of(i * 8, 8), 8)
        coded = sent_ref[3, sl, :]
        master = jnp.maximum(coded - 0.5, 0.0).astype(jnp.int32)
        normal = [sent_ref[c, sl, :] for c in range(3)]
        found = lookup(state_rows(x_ref, v_ref, rows), master)
        gap = sent_ref[4, sl, :] - sum(found[c] * normal[c] for c in range(3))
        closing = sent_ref[5, sl, :] - sum(found[3 + c] * normal[c] for c in range(3))
        z = -gap / GAP_WIDTH
        soft = jnp.maximum(z, 0.0) + jnp.log1p(jnp.exp(-jnp.abs(z)))
        push = PENALTY * GAP_WIDTH * soft - CONTACT_DAMP * closing
        push = jnp.where(coded > 0.5, push, 0.0)
        push_ref[sl, :] = push
        total[...] += scatter_tile(master, [-push * normal[c] for c in range(3)], rows, 2)
        return carry

    lax.fori_loop(0, push_ref.shape[0] // 8, step, 0, unroll=4)
    for c, value in enumerate(unstack(total[...], 3, rows, 2)):
        force_ref[c] = value


def finish_body(x_ref, v_ref, as_ref, ext_ref, mass_ref, accel_ref, force_ref, push_ref, slot_ref,
                slave_ref, normal_ref, part_ref, nv_ref, sums_ref, vals, total):
    rows = x_ref.shape[1]
    push_rows = [[push_ref[r : r + 1, :]] for r in range(push_ref.shape[0])]
    acc = None
    for t in range(0, slave_ref.shape[0], 8):
        sl = slice(t, t + 8)
        push = lookup(push_rows, slot_ref[sl, :])[0]
        got = scatter_tile(slave_ref[sl, :], [push * normal_ref[c, sl, :] for c in range(3)],
                           rows, 2)
        acc = got if acc is None else acc + got
    slave_force = unstack(acc, 3, rows, 2)
    mass = mass_ref[...]
    x = [x_ref[c] for c in range(3)]
    net = []
    for c in range(3):
        force = force_ref[c] + slave_force[c]
        nv_ref[c] = v_ref[c] + TIME_STEP * force / mass
        net.append(ext_ref[c] - as_ref[c] + force - mass * accel_ref[c])
    turned = [x[1] * net[2] - x[2] * net[1], x[2] * net[0] - x[0] * net[2],
              x[0] * net[1] - x[1] * net[0]]
    for i, value in enumerate([mass] + [mass * x[c] for c in range(3)] + net + turned):
        vals[i] = value
    part_rows = sums_ref.shape[1]
    total[...] = jnp.zeros_like(total)

    def step(i, carry):
        sl = pl.ds(pl.multiple_of(i * 8, 8), 8)
        part = part_ref[sl, :]
        total[...] += scatter_tile(part, [vals[k, sl, :] for k in range(10)], part_rows, 3)
        return carry

    lax.fori_loop(0, rows // 8, step, 0, unroll=2)
    for k, value in enumerate(unstack(total[...], 10, part_rows, 3)):
        sums_ref[k] = value


def coords(index):
    return {"dom": index}


def greet(peers):
    barrier = pltpu.get_barrier_semaphore()
    for peer in peers:
        pl.semaphore_signal(barrier, inc=1, device_id=coords(peer),
                            device_id_type=pl.DeviceIdType.MESH)
    pl.semaphore_wait(barrier, len(peers))


def send(source, target, send_sem, recv_sem, peer):
    return pltpu.make_async_remote_copy(
        src_ref=source, dst_ref=target, send_sem=send_sem, recv_sem=recv_sem,
        device_id=coords(peer), device_id_type=pl.DeviceIdType.MESH)


def exchange_body(neighbours, own_ref, got_ref, send_sem, recv_sem):
    me = lax.axis_index("dom")
    peers = [me + (1 - 2 * ((me // 2**b) % 2)) * 2**b for b in range(neighbours)]
    greet(peers)
    copies = [send(own_ref.at[b], got_ref.at[b], send_sem.at[b], recv_sem.at[b], peers[b])
              for b in range(neighbours)]
    for copy in copies:
        copy.start()
    for copy in copies:
        copy.wait()


def swap_body(domains, in_ref, out_ref, send_sem, recv_sem, own_sem):
    me = lax.axis_index("dom")
    own = pltpu.make_async_copy(in_ref.at[me], out_ref.at[me], own_sem)
    own.start()
    peers = [(me + apart) % domains for apart in range(1, domains)]
    greet(peers)
    copies = [send(in_ref.at[peer], out_ref.at[me], send_sem.at[i], recv_sem.at[i], peer)
              for i, peer in enumerate(peers)]
    for copy in copies:
        copy.start()
    for copy in copies:
        copy.wait()
    own.wait()


def bit_groups(domains):
    bits = domains.bit_length() - 1
    groups, low = [], 0
    while low < bits:
        width = min(3, bits - low)
        if bits - low == 4:
            width = 2
        groups.append((low, width))
        low += width
    return groups


def total_body(domains, in_ref, out_ref, *scratch):
    groups = bit_groups(domains)
    held, partial, (send_sem, recv_sem, own_sem) = (
        scratch[:len(groups)], scratch[len(groups):2 * len(groups) - 1], scratch[-3:])
    me = lax.axis_index("dom")
    plans = []
    for low, width in groups:
        size = 2**width
        digit = (me // 2**low) % size
        base = me - digit * 2**low
        plans.append((digit, [base + ((digit + o) % size) * 2**low for o in range(1, size)]))
    greet([peer for _, peers in plans for peer in peers])
    source = in_ref
    place = 0
    for g, (digit, peers) in enumerate(plans):
        own = pltpu.make_async_copy(source, held[g].at[digit], own_sem.at[g])
        copies = [own]
        for i, peer in enumerate(peers):
            copies.append(send(source, held[g].at[digit], send_sem.at[place + i],
                               recv_sem.at[place + i], peer))
        place += len(peers)
        for copy in copies:
            copy.start()
        for copy in copies:
            copy.wait()
        value = held[g][0]
        for k in range(1, len(peers) + 1):
            value = value + held[g][k]
        if g + 1 < len(plans):
            partial[g][...] = value
            source = partial[g]
        else:
            out_ref[...] = value


VMEM = pl.BlockSpec(memory_space=pltpu.VMEM)
SMEM = pl.BlockSpec(memory_space=pltpu.SMEM)


def call(body, outs, scratch, specs, name, collective=None):
    return pl.pallas_call(
        body,
        out_shape=outs,
        in_specs=specs,
        out_specs=[VMEM] * len(outs),
        scratch_shapes=scratch,
        name=name,
        compiler_params=pltpu.CompilerParams(
            vmem_limit_bytes=48 * 2**20, collective_id=collective,
            has_side_effects=collective is not None),
    )


def cross_product(left, right):
    return jnp.stack([
        left[1] * right[2] - left[2] * right[1],
        left[2] * right[0] - left[0] * right[2],
        left[0] * right[1] - left[1] * right[0],
    ])


def f32(*shape):
    return jax.ShapeDtypeStruct(shape, F32)


def by_owner(payload, domains):
    count, slot_rows, _ = payload.shape
    each = slot_rows // domains
    return payload.reshape(count, domains, each, L).transpose(1, 0, 2, 3).reshape(
        domains, count * each, L)


def to_slots(payload, count):
    domains, each, _ = payload.shape
    each = each // count
    return payload.reshape(domains, count, each, L).transpose(1, 0, 2, 3).reshape(
        count, domains * each, L)


def swap(payload, domains, collective):
    return call(
        functools.partial(swap_body, domains), [f32(*payload.shape)],
        [pltpu.SemaphoreType.DMA((domains,))] * 2 + [pltpu.SemaphoreType.DMA], [VMEM], "swap",
        collective)(payload)[0]


def exchange(own):
    neighbours = own.shape[0]
    return call(
        functools.partial(exchange_body, neighbours), [f32(*own.shape)],
        [pltpu.SemaphoreType.DMA((neighbours,))] * 2, [VMEM], "exchange", 0)(own)[0]


def total_over(sums, domains):
    groups = bit_groups(domains)
    count = sum(2**width - 1 for _, width in groups)
    return call(
        functools.partial(total_body, domains), [f32(*sums.shape)],
        [pltpu.VMEM((2**width,) + sums.shape, F32) for _, width in groups]
        + [pltpu.VMEM(sums.shape, F32)] * (len(groups) - 1)
        + [pltpu.SemaphoreType.DMA((count,))] * 2 + [pltpu.SemaphoreType.DMA((len(groups),))],
        [VMEM], "total", 1)(sums)[0]


def per_device(rest_pos, displacement, velocity, ext_force, node_mass, body_accel, connectivity,
               elem_material, stiffness, shared_nodes, contact_slave, contact_owner,
               contact_master, contact_normal, part_of_node, part_mass, part_center,
               part_inertia):
    domains = lax.axis_size("dom")
    neighbours, shared_count = shared_nodes.shape[1:]
    nodes = displacement.shape[1]
    rows = nodes // L
    elems = connectivity.shape[1]
    blocks = elems // L
    contacts = contact_slave.shape[0]
    tiles = contacts // L
    cap = -(-(4 * contacts // domains) // L) * L
    slot_rows = domains * cap // L
    part_rows = -(-PARTS_SIZE // L)

    corners = (connectivity + jnp.arange(elems, dtype=jnp.int32)[None, :]) % nodes
    u = displacement.reshape(3, rows, L)
    v = velocity.reshape(3, rows, L)
    ext = ext_force.reshape(3, rows, L)
    rest = rest_pos.reshape(3, rows, L)
    mass = node_mass.reshape(rows, L)
    shared = jnp.concatenate(
        [shared_nodes[0], jnp.zeros((8 - neighbours, shared_count), jnp.int32)], 0)
    k_hi = lax.reduce_precision(stiffness, 8, 7)
    k_lo = stiffness - k_hi
    matrix = jnp.concatenate(
        [k_hi, k_hi, k_lo, jnp.zeros(stiffness.shape[:2] + (8,), F32)], 2).astype(BF16)
    materials = stiffness.shape[0]
    pick = (elem_material[:, None] == jnp.arange(materials, dtype=jnp.int32)[None]).astype(BF16)
    matrix = jnp.dot(pick, matrix.reshape(materials, -1), preferred_element_type=F32)
    matrix = matrix.astype(BF16).reshape(blocks, 24, 80)

    owner = contact_owner.reshape(tiles, L)
    master = contact_master.reshape(tiles, L)
    slave = contact_slave.reshape(tiles, L)
    normal = contact_normal.reshape(3, tiles, L)
    slot, early = call(
        functools.partial(slots_body, domains=domains, cap=cap),
        [jax.ShapeDtypeStruct((tiles, L), jnp.int32), f32(4, slot_rows, L)], [],
        [VMEM] * 3, "slots")(owner, master, normal)

    node_shape = f32(3, rows, L)
    own_shape = f32(neighbours, 8, L)
    scratch = [pltpu.VMEM((3, rows, L), F32), pltpu.VMEM((6 * rows, L), F32)]
    received = internal = None
    for cycle in range(CYCLES):
        if cycle == 0:
            internal, own = call(
                functools.partial(elem_body, True, neighbours), [node_shape, own_shape], scratch,
                [VMEM] * 5, "elements")(u, v, corners, shared, matrix)
        else:
            internal, own, u, v = call(
                functools.partial(elem_body, False, neighbours),
                [node_shape, own_shape, node_shape, node_shape], scratch,
                [VMEM] * 9 + [SMEM], "elements")(
                    u, v, corners, shared, matrix, internal, received, ext, mass, body_accel)
        received = exchange(own)

    x, v, assembled, late = call(
        functools.partial(project_body, neighbours),
        [node_shape, node_shape, node_shape, f32(2, slot_rows, L)], [],
        [VMEM] * 7 + [SMEM] + [VMEM] * 4, "project")(
            u, v, shared, internal, received, ext, mass, body_accel, rest, slave, slot, normal)
    sent = jnp.concatenate([early, late], 0)
    sent = to_slots(swap(by_owner(sent, domains), domains, 3), 6)
    push, force = call(
        push_body, [f32(slot_rows, L), node_shape], [pltpu.VMEM((6 * rows, L), F32)],
        [VMEM] * 3, "push")(x, v, sent)
    push = to_slots(swap(by_owner(push[None], domains), domains, 4), 1)[0]
    nodal_velocity, sums = call(
        finish_body, [node_shape, f32(10, part_rows, L)],
        [pltpu.VMEM((10, rows, L), F32), pltpu.VMEM((30 * max(part_rows, 16), L), F32)],
        [VMEM] * 5 + [SMEM] + [VMEM] * 6, "finish")(
            x, v, assembled, ext, mass, body_accel, force, push, slot, slave, normal,
            part_of_node.reshape(rows, L))
    totals = total_over(sums, domains).reshape(10, part_rows * L)[:, :PARTS_SIZE]
    mass_total = part_mass + totals[0]
    centre = (part_mass[None] * part_center + totals[1:4]) / mass_total[None]
    force_sum = totals[4:7]
    torque = totals[7:10] - cross_product(centre, force_sum)
    part_motion = jnp.concatenate([force_sum / mass_total[None], torque / part_inertia], 0)
    return nodal_velocity.reshape(3, nodes), part_motion


def solution(mesh):
    placed = (
        P(None, "dom"), P(None, "dom"), P(None, "dom"), P(None, "dom"), P("dom"), P(),
        P(None, "dom"), P("dom"), P(), P("dom", None, None), P("dom"), P("dom", None), P("dom"),
        P(None, "dom"), P("dom"), P(), P(), P(),
    )
    return jax.shard_map(
        per_device, mesh=mesh, in_specs=placed, out_specs=(P(None, "dom"), P()), check_vma=False
    )
```
